256 devices in a mesh: grp: 8 (over z_hi, x), dev: 32 (over y, z_lo, core).
Axes of the slice: x: 4, y: 4, z: 8 (z_hi: 2, z_lo: 4; z = z_hi * 4 + z_lo), core: 2. Of those that a mesh axis runs over, the one named last changes fastest.
Arguments:
- step_number: int32 [], replicated, may hold values from 0 to 999
- power_maps: bfloat16 [2048, 64, 128], P(('grp', 'dev')), may hold values from -6 to 6
- heat_maps: bfloat16 [2048, 1024], P(('grp', 'dev')), may hold values from -6 to 6
- home_table: int32 [8, 256], P('grp'), may hold values from 0 to 255, as said below
- requests: int32 [256, 32], P(('grp', 'dev')), may hold values from 0 to 255, as said below
- counts: int32 [256], P(('grp', 'dev')), may hold values from 1 to 32, as said below
- stem_weight: float32 [256, 128, 256], P(('grp', 'dev')), may hold values from -0.5 to 0.5
- conv_weight: float32 [256, 2, 2304, 256], P(('grp', 'dev')), may hold values from -0.125 to 0.125
- head_weight: float32 [256, 16, 256], P(('grp', 'dev')), may hold values from -0.375 to 0.375
- biases: float32 [256, 3, 256], P(('grp', 'dev')), may hold values from -3 to 3
Outputs:
- new_stem: float32 [256, 128, 256], P(('grp', 'dev'))
- new_conv: float32 [256, 2, 2304, 256], P(('grp', 'dev'))
- new_head: float32 [256, 16, 256], P(('grp', 'dev'))
- new_biases: float32 [256, 3, 256], P(('grp', 'dev'))
- grad_stem: bfloat16 [256, 128, 256], P(('grp', 'dev'))
- grad_conv: bfloat16 [256, 2, 2304, 256], P(('grp', 'dev'))
- grad_head: bfloat16 [256, 16, 256], P(('grp', 'dev'))
- grad_biases: bfloat16 [256, 3, 256], P(('grp', 'dev'))
The draws below stay inside these ranges and needn't reach their ends.
Inputs may be any that keep to these rules, and one draw needn't show every extreme that they name: Each row is a permutation; sample s of group g is stored by dev index home_table[g, s] // 8 as its local sample home_table[g, s] % 8. Among the live requests of one device (its first counts entries) at most 2 are stored by any one dev index; in every group some device has exactly 2 from one dev index. `counts`: in every group some device has 32 live requests.
All inputs are finite; a program needn't handle non-finite values.
Results may differ from the reference program's by a relative error of at most 0.024.
The reference program's roundings to bfloat16 on the way (of `stem_act`, `inner_act` and `block_out`) count: a program that leaves them out, or rounds other values in their place, can miss the bound.
Values may be sent and summed in bfloat16 or wider, within the bound.
No kernel may reach another device: no remote copies, remote signals or barrier semaphores. Data moves between devices by JAX's collectives and lax.ppermute only.
A program may use at most 128 MiB of HBM per device.

```python
import jax
import jax.numpy as jnp
from jax import lax

C = 256
FEAT = 128
OUTPIX = 16
PH = 8
PW = 8
S_DEV = 8
REQ = 32
GROUPS = 8
PEERS = 32
GSAMPLES = 256
DEVICES = 256


def make_tables(key):
    folded = jax.random.fold_in(key, 11)
    key_home, key_owner, key_local, key_second, key_first, key_other, key_order, key_full = jax.random.split(folded, 8)
    home_table = jax.vmap(lambda single: jax.random.permutation(single, GSAMPLES))(jax.random.split(key_home, GROUPS)).astype(jnp.int32)
    inverse = jnp.argsort(home_table, axis=1).astype(jnp.int32)
    half_req = REQ // 2
    owner_perm = jax.vmap(lambda single: jax.random.permutation(single, PEERS))(jax.random.split(key_owner, DEVICES))[:, :half_req]
    owner_list = jnp.concatenate([owner_perm, owner_perm], axis=1).astype(jnp.int32)
    local_base = jax.random.randint(key_local, (DEVICES, half_req), 0, S_DEV)
    second = (local_base + 1 + jax.random.randint(key_second, (DEVICES, half_req), 0, S_DEV - 1)) % S_DEV
    local_list = jnp.concatenate([local_base, second], axis=1).astype(jnp.int32)
    shuffle = jax.vmap(lambda single: jax.random.permutation(single, REQ))(jax.random.split(key_order, DEVICES))
    owner_list = jnp.take_along_axis(owner_list, shuffle, axis=1)
    local_list = jnp.take_along_axis(local_list, shuffle, axis=1)
    position = owner_list * S_DEV + local_list
    group_of = jnp.arange(DEVICES, dtype=jnp.int32) // PEERS
    requests = jnp.take_along_axis(inverse[group_of], position, axis=1).astype(jnp.int32)
    first_draw = jax.random.randint(key_first, (DEVICES,), half_req, REQ + 1)
    other_draw = jax.random.randint(key_other, (DEVICES,), half_req, REQ + 1)
    chosen = jax.random.randint(key_full, (GROUPS,), 0, PEERS)
    counts = jnp.where(jnp.arange(DEVICES, dtype=jnp.int32) % PEERS == chosen[group_of], REQ, jnp.maximum(first_draw, other_draw))
    return (home_table, requests, counts.astype(jnp.int32))


def draw_home_table(key, part):
    return make_tables(key)[0]


def draw_requests(key, part):
    return make_tables(key)[1]


def draw_counts(key, part):
    return make_tables(key)[2]


def steps_of(rng, shape, cuts, least, largest):
    def one(axis_at, parts):
        heights = jax.random.uniform(jax.random.fold_in(jax.random.fold_in(rng, 6), axis_at), (parts,), jnp.float32, least / len(cuts), largest / len(cuts))
        return jnp.repeat(jnp.exp(heights), shape[axis_at] // parts).reshape((-1,) + (1,) * (len(shape) - axis_at - 1))

    gain = one(*cuts[0])
    for cut in cuts[1:]:
        gain = gain * one(*cut)
    return gain


def scatter_about(key, extent, scale, most, pieces=(), kind=jnp.bfloat16):
    result = jax.random.normal(key, extent, jnp.float32) * scale
    if len(pieces) > 0:
        result = steps_of(key, extent, pieces, -0.22, 0.18) * result
    return jnp.clip(result, min=-most, max=most).astype(kind)


def setup_inputs(seed: int = 0) -> dict:
    arg_keys = jax.random.split(jax.random.key(seed), 11)
    step_number = jax.random.randint(arg_keys[0], (), 0, 1000).astype(jnp.int32)
    power_maps = scatter_about(arg_keys[1], (DEVICES * S_DEV, PH * PW, FEAT), 1.0, 6.0, ((0, 256),))
    heat_maps = scatter_about(arg_keys[2], (DEVICES * S_DEV, PH * PW * OUTPIX), 1.0, 6.0, ((0, 256),))
    home_table = draw_home_table(jax.random.fold_in(arg_keys[10], 71), 0)
    requests = draw_requests(jax.random.fold_in(arg_keys[10], 71), 0)
    counts = draw_counts(jax.random.fold_in(arg_keys[10], 71), 0)
    stem_weight = scatter_about(arg_keys[6], (DEVICES, FEAT, C), FEAT ** -0.5, 0.5, ((0, 256),), jnp.float32)
    conv_weight = scatter_about(arg_keys[7], (DEVICES, 2, 9 * C, C), (9 * C) ** -0.5, 0.125, ((0, 256),), jnp.float32)
    head_weight = scatter_about(arg_keys[8], (DEVICES, OUTPIX, C), C ** -0.5, 0.375, ((0, 256),), jnp.float32)
    biases = scatter_about(arg_keys[9], (DEVICES, 3, C), 0.5, 3.0, ((0, 256),), jnp.float32)
    return {"step_number": step_number, "power_maps": power_maps, "heat_maps": heat_maps, "home_table": home_table, "requests": requests, "counts": counts, "stem_weight": stem_weight, "conv_weight": conv_weight, "head_weight": head_weight, "biases": biases}


LEARN_RATE = 0.1

def conv_three(activation, weight, height, width):
    batch_size, positions, channels = activation.shape
    grid_map = activation.reshape(batch_size, height, width, channels)
    padded = jnp.pad(grid_map, ((0, 0), (1, 1), (1, 1), (0, 0)))
    columns = jnp.concatenate([padded[:, row_shift:row_shift + height, col_shift:col_shift + width, :] for row_shift in range(3) for col_shift in range(3)], axis=3)
    product = jnp.dot(columns.reshape(batch_size * positions, 9 * channels), weight, preferred_element_type=jnp.float32)
    return product.reshape(batch_size, positions, channels)

def batch_loss(params, power_maps, heat_maps, alive_mask, sample_count, height, width):
    stem_weight, conv_weight, head_weight, biases = params
    batch_size, positions, features = power_maps.shape
    channels = stem_weight.shape[1]
    stem_pre = jnp.dot(power_maps.reshape(batch_size * positions, features), stem_weight.astype(jnp.bfloat16), preferred_element_type=jnp.float32) + biases[0]
    stem_act = jax.nn.relu(stem_pre).astype(jnp.bfloat16).reshape(batch_size, positions, channels)
    inner_act = jax.nn.relu(conv_three(stem_act, conv_weight[0].astype(jnp.bfloat16), height, width) + biases[1]).astype(jnp.bfloat16)
    branch_out = conv_three(inner_act, conv_weight[1].astype(jnp.bfloat16), height, width) + biases[2]
    block_out = jax.nn.relu(stem_act.astype(jnp.float32) + branch_out).astype(jnp.bfloat16)
    predicted = lax.dot_general(block_out.reshape(batch_size * positions, channels), head_weight.astype(jnp.bfloat16), (((1,), (1,)), ((), ())), preferred_element_type=jnp.float32).reshape(batch_size, -1)
    error_map = (predicted - heat_maps.astype(jnp.float32)) * alive_mask[:, None]
    return jnp.sum(error_map * error_map) / (sample_count * error_map.shape[1])

def reference(step_number, power_maps, heat_maps, home_table, requests, counts, stem_weight, conv_weight, head_weight, biases):
    bit_count = DEVICES.bit_length() - 1
    flip_mask = jnp.left_shift(jnp.int32(1), (step_number % bit_count).astype(jnp.int32))

    def per_device(device):
        group_of = device // PEERS
        position = jnp.take(home_table[group_of], requests[device], axis=0)
        source_rows = (group_of * GSAMPLES + position).astype(jnp.int32)
        batch_maps = jnp.take(power_maps, source_rows, axis=0)
        batch_heat = jnp.take(heat_maps, source_rows, axis=0)
        alive_mask = (jnp.arange(REQ, dtype=jnp.int32) < counts[device]).astype(jnp.float32)
        params = (stem_weight[device], conv_weight[device], head_weight[device], biases[device])
        gradients = jax.grad(batch_loss)(params, batch_maps, batch_heat, alive_mask, counts[device].astype(jnp.float32), PH, PW)
        partner = jnp.bitwise_xor(device, flip_mask)
        theirs_all = (stem_weight[partner], conv_weight[partner], head_weight[partner], biases[partner])
        updated = tuple((0.5 * (mine + theirs) - LEARN_RATE * gradient for mine, theirs, gradient in zip(params, theirs_all, gradients)))
        return updated + tuple((gradient.astype(jnp.bfloat16) for gradient in gradients))
    results = lax.map(per_device, jnp.arange(DEVICES, dtype=jnp.int32))
    return (results[0], results[1], results[2], results[3], results[4], results[5], results[6], results[7])
```

```python
import functools

import jax
import jax.numpy as jnp
from jax import lax
from jax.experimental import pallas as pl
from jax.experimental.pallas import tpu as pltpu
from jax.sharding import PartitionSpec as P

bf16 = jnp.bfloat16
f32 = jnp.float32
NT = (((1,), (1,)), ((), ()))
TN = (((0,), (0,)), ((), ()))
ROW_STEM = 4608
ROW_HEAD = 4736
PACKED = 4768


def dot(a, b):
    return jnp.dot(a, b, preferred_element_type=f32)


def main_kernel(
    count_ref, scale_ref, sel_ref, got_ref, wa_hbm, wb_hbm, bias_ref, conv_hbm, stem_ref, head_ref,
    gconv_hbm, base_hbm, gstem_ref, ghead_ref, gbias_ref, bstem_ref, bhead_ref, bbias_ref,
    wb, mine, gb, x_s, heat_s, a0p, a1p, a2, d2p, d1p, a0t, a1t, whe, wsem, msem, osem, gsem,
    *, U, stage):
    wcopies = []
    na = wa_hbm.shape[0]
    for k, (src, lo, n) in enumerate((
        (wb_hbm, ROW_STEM, PACKED - ROW_STEM), (wa_hbm, 0, na), (wb_hbm, na, 2304 - na), (wb_hbm, 2304, 2304),
    )):
        at = lo if src is wa_hbm else lo - na
        c = pltpu.make_async_copy(src.at[pl.ds(at, n)], wb.at[pl.ds(lo, n)], wsem.at[k])
        c.start()
        wcopies.append(c)
    mcopies = []
    for k in range(2):
        c = pltpu.make_async_copy(conv_hbm.at[pl.ds(k * 2304, 2304)], mine.at[k], msem.at[k])
        c.start()
        mcopies.append(c)

    for buf in (a0p, a1p, d2p, d1p):
        z = jnp.zeros((320, 256), bf16)
        buf[0] = z
        buf[9] = z

    @pl.loop(1, 9)
    def _(u):
        z = jnp.zeros((32, 256), bf16)
        for buf in (a0p, a1p, d2p, d1p):
            buf[u, 0:32] = z
            buf[u, 288:320] = z

    sel = sel_ref[...]

    @pl.loop(0, 8)
    def _(u):
        blk = got_ref[:, pl.ds(pl.multiple_of(u * 1024, 1024), 1024)]
        r = dot(sel, blk).astype(bf16)
        for v in range(8):
            x_s[u, v * 32:(v + 1) * 32, :] = r[:, v * 128:(v + 1) * 128]
        hb = got_ref[:, pl.ds(pl.multiple_of(8192 + u * 128, 128), 128)]
        heat_s[pl.ds(pl.multiple_of(u * 32, 32), 32), :] = dot(sel, hb)

    wcopies[0].wait()
    ws = wb[ROW_STEM:ROW_STEM + 128, :]
    wh = wb[ROW_HEAD:ROW_HEAD + 16, :]
    whe[...] = jnp.zeros_like(whe)
    for v in range(8):
        whe[v * 16:(v + 1) * 16, v * 256:(v + 1) * 256] = wh

    b0 = bias_ref[0:1, :]
    b1 = bias_ref[1:2, :]
    b2 = bias_ref[2:3, :]

    @pl.loop(0, 8)
    def _(u):
        pre = dot(x_s[u], ws) + b0
        act = jnp.maximum(pre, 0.0).astype(bf16)
        a0p[u + 1, 32:288, :] = act
        a0t[:, pl.ds(pl.multiple_of(u * 256, 256), 256)] = act.T

    wcopies[1].wait()
    wcopies[2].wait()

    def slabs(buf, u, flip):
        rows = []
        for s in range(U):
            taps = []
            for i in range(3):
                for j in range(3):
                    ii, jj = (2 - i, 2 - j) if flip else (i, j)
                    taps.append(buf[u + s + ii, jj * 32:jj * 32 + 256, :])
            rows.append(jnp.concatenate(taps, axis=1))
        return rows[0] if U == 1 else jnp.concatenate(rows, axis=0)

    if stage >= 1:
        @pl.loop(0, 8 // U)
        def _(k):
            u = k * U
            pre = dot(slabs(a0p, u, False), wb[0:2304, :]) + b1
            act = jnp.maximum(pre, 0.0).astype(bf16)
            for s in range(U):
                part = act[s * 256:(s + 1) * 256]
                a1p[u + s + 1, 32:288, :] = part
                a1t[:, pl.ds(pl.multiple_of((u + s) * 256, 256), 256)] = part.T

    wcopies[3].wait()
    if stage >= 2:
        @pl.loop(0, 8 // U)
        def _(k):
            u = k * U
            pre = dot(slabs(a1p, u, False), wb[2304:4608, :]) + b2
            for s in range(U):
                act = jnp.maximum(pre[s * 256:(s + 1) * 256] + a0p[u + s + 1, 32:288, :].astype(f32), 0.0).astype(bf16)
                a2[u + s] = act

    count = count_ref[0]
    scale = scale_ref[0]
    if stage >= 3:
        a2cat = jnp.concatenate([a2[:, v * 32:(v + 1) * 32, :].reshape(256, 256) for v in range(8)], axis=1)
        pred = lax.dot_general(a2cat, whe[...], NT, preferred_element_type=f32)
        row = lax.broadcasted_iota(jnp.int32, (256, 128), 0)
        alive = (row & 31) < count
        err = jnp.where(alive, (pred - heat_s[...]) * scale, 0.0).astype(bf16)
        acc2 = jnp.zeros((1, 256), f32)
        gh = jnp.zeros((16, 256), f32)
        errt = err.T
        for v in range(8):
            a2v = a2[:, v * 32:(v + 1) * 32, :].reshape(256, 256)
            da = dot(err, whe[:, v * 256:(v + 1) * 256])
            da = jnp.where(a2v > 0, da, 0.0).astype(bf16)
            acc2 = acc2 + jnp.sum(da.astype(f32), axis=0, keepdims=True)
            d2p[1:9, (v + 1) * 32:(v + 2) * 32, :] = da.reshape(8, 32, 256)
            gh = gh + dot(errt[v * 16:(v + 1) * 16], a2v)
        ghead_ref[...] = gh.astype(bf16)
        bhead_ref[...] = 0.5 * head_ref[...] - 0.1 * gh
        gbias_ref[2:3, :] = acc2.astype(bf16)
        bbias_ref[2:3, :] = 0.5 * b2 - 0.1 * acc2

    def dslabs_dot(buf, u, row0):
        out = None
        for i in range(3):
            for j in range(3):
                ii, jj = 2 - i, 2 - j
                if U == 1:
                    lhs = buf[u + ii, jj * 32:jj * 32 + 256, :]
                else:
                    lhs = jnp.concatenate([buf[u + s + ii, jj * 32:jj * 32 + 256, :] for s in range(U)], axis=0)
                w = wb[row0 + (3 * i + j) * 256: row0 + (3 * i + j + 1) * 256, :]
                t = lax.dot_general(lhs, w, NT, preferred_element_type=f32)
                out = t if out is None else out + t
        return out

    if stage >= 4:
        def step1(k, acc):
            u = k * U
            da = dslabs_dot(d2p, u, 2304)
            for s in range(U):
                d = jnp.where(a1p[u + s + 1, 32:288, :] > 0, da[s * 256:(s + 1) * 256], 0.0).astype(bf16)
                d1p[u + s + 1, 32:288, :] = d
                acc = acc + jnp.sum(d.astype(f32), axis=0, keepdims=True)
            return acc
        acc1 = lax.fori_loop(0, 8 // U, step1, jnp.zeros((1, 256), f32))
        gbias_ref[1:2, :] = acc1.astype(bf16)
        bbias_ref[1:2, :] = 0.5 * b1 - 0.1 * acc1

    def wgrad(which, at, dp):
        @pl.loop(0, 9)
        def _(t):
            ii = 2 - t // 3
            jj = 2 - t % 3
            lhs = at[...]
            rhs = jnp.concatenate([dp[u + ii, pl.ds(pl.multiple_of(jj * 32, 32), 256), :] for u in range(8)], axis=0)
            g = dot(lhs, rhs)
            r = pl.ds(pl.multiple_of(t * 256, 256), 256)
            gb[which, r, :] = g.astype(bf16)
            mine[which, r, :] = 0.5 * mine[which, r, :] - 0.1 * g
            pltpu.make_async_copy(gb.at[which, r], gconv_hbm.at[which, r], gsem.at[which, t]).start()
            pltpu.make_async_copy(mine.at[which, r], base_hbm.at[which, r], osem.at[which, t]).start()

    mcopies[0].wait()
    mcopies[1].wait()
    if stage >= 5:
        wgrad(1, a1t, d2p)

    if stage >= 6:
        def step0(k, carry):
            acc, gs = carry
            u = k * U
            da = dslabs_dot(d1p, u, 0)
            for s in range(U):
                d = da[s * 256:(s + 1) * 256] + d2p[u + s + 1, 32:288, :].astype(f32)
                d = jnp.where(a0p[u + s + 1, 32:288, :] > 0, d, 0.0).astype(bf16)
                acc = acc + jnp.sum(d.astype(f32), axis=0, keepdims=True)
                gs = gs + lax.dot_general(x_s[u + s], d, TN, preferred_element_type=f32)
            return acc, gs
        acc0, gs = lax.fori_loop(0, 8 // U, step0, (jnp.zeros((1, 256), f32), jnp.zeros((128, 256), f32)))
        gbias_ref[0:1, :] = acc0.astype(bf16)
        bbias_ref[0:1, :] = 0.5 * b0 - 0.1 * acc0
        gstem_ref[...] = gs.astype(bf16)
        bstem_ref[...] = 0.5 * stem_ref[...] - 0.1 * gs

    if stage >= 7:
        wgrad(0, a0t, d1p)

    for which in ((1, 0) if stage >= 7 else (1,) if stage >= 5 else ()):
        for t in range(9):
            r = pl.ds(t * 256, 256)
            pltpu.make_async_copy(gb.at[which, r], gconv_hbm.at[which, r], gsem.at[which, t]).wait()
            pltpu.make_async_copy(mine.at[which, r], base_hbm.at[which, r], osem.at[which, t]).wait()


def main_call(count, scale, sel, got, wa, wb, bias, conv, stem, head, U=2, stage=9):
    vm = pl.BlockSpec(memory_space=pltpu.VMEM)
    sm = pl.BlockSpec(memory_space=pltpu.SMEM)
    hb = pl.BlockSpec(memory_space=pl.ANY)
    S = jax.ShapeDtypeStruct
    pad = pltpu.VMEM((10, 320, 256), bf16)
    return pl.pallas_call(
        functools.partial(main_kernel, U=U, stage=stage),
        out_shape=(S((2, 2304, 256), bf16), S((2, 2304, 256), f32), S((128, 256), bf16), S((16, 256), bf16), S((3, 256), bf16),
                   S((128, 256), f32), S((16, 256), f32), S((3, 256), f32)),
        in_specs=[sm, sm, vm, vm, hb, hb, vm, hb, vm, vm],
        out_specs=(hb, hb, vm, vm, vm, vm, vm, vm),
        scratch_shapes=[
            pltpu.VMEM((PACKED, 256), bf16), pltpu.VMEM((2, 2304, 256), f32), pltpu.VMEM((2, 2304, 256), bf16),
            pltpu.VMEM((8, 256, 128), bf16), pltpu.VMEM((256, 128), f32), pad, pad, pltpu.VMEM((8, 256, 256), bf16), pad, pad,
            pltpu.VMEM((256, 2048), bf16), pltpu.VMEM((256, 2048), bf16), pltpu.VMEM((128, 2048), bf16),
            pltpu.SemaphoreType.DMA((4,)), pltpu.SemaphoreType.DMA((2,)), pltpu.SemaphoreType.DMA((2, 9)), pltpu.SemaphoreType.DMA((2, 9)),
        ],
        compiler_params=pltpu.CompilerParams(vmem_limit_bytes=48 * 1024 * 1024),
        cost_estimate=pl.CostEstimate(flops=16_000_000_000, bytes_accessed=16_000_000, transcendentals=0),
    )(count, scale, sel, got, wa, wb, bias, conv, stem, head)


ROWS_A = 1280
ROWS_B = PACKED - ROWS_A
BOTH = ("grp", "dev")


def route_kernel(count_ref, zpos_ref, req_ref, home_ref, asked_ref, sel_ref):
    req = req_ref[...]
    lane = lax.broadcasted_iota(jnp.int32, (32, 256), 1)
    pos = jnp.sum(jnp.where(lane == req, home_ref[...], 0), axis=1, keepdims=True)
    owner = pos >> 3
    column = (owner >> 3) * 2 + (owner & 1)
    row = (((owner >> 1) & 3) ^ zpos_ref[0]) * 8 + (pos & 7)
    me = lax.broadcasted_iota(jnp.int32, (32, 1), 0)
    live = me < count_ref[0]
    column_f = column.astype(f32)
    across = jnp.broadcast_to(column_f, (32, 128)).T[0:32, :]
    i = lax.broadcasted_iota(jnp.int32, (32, 32), 0)
    j = lax.broadcasted_iota(jnp.int32, (32, 32), 1)
    earlier = (across == column_f) & (j < i) & (j < count_ref[0])
    rank = jnp.sum(earlier.astype(jnp.int32), axis=1, keepdims=True)
    rank = jnp.minimum(rank, 7)
    slot = column * 8 + rank
    lane64 = lax.broadcasted_iota(jnp.int32, (32, 64), 1)
    sel_ref[...] = jnp.where((lane64 == slot) & live, 1.0, 0.0).astype(bf16)
    lane8 = lax.broadcasted_iota(jnp.int32, (32, 8), 1)
    left = jnp.where((lane8 == column) & live, 1.0, 0.0).astype(bf16)
    right = jnp.where(lane8 == rank, (row + 1).astype(f32), 0.0).astype(bf16)
    asked = lax.dot_general(left, right, TN, preferred_element_type=f32)
    asked_ref[...] = asked.astype(jnp.int32) - 1


def route(count, zpos, req, home):
    vm = pl.BlockSpec(memory_space=pltpu.VMEM)
    sm = pl.BlockSpec(memory_space=pltpu.SMEM)
    S = jax.ShapeDtypeStruct
    return pl.pallas_call(
        route_kernel,
        out_shape=(S((8, 8), jnp.int32), S((32, 64), bf16)),
        in_specs=[sm, sm, vm, vm],
        out_specs=(vm, vm),
    )(count, zpos, req, home)


CHUNKS = ((0, 640), (640, 640), (1280, 1152), (2432, 1152), (3584, 1024))


def pack_kernel(conv_hbm, stem_ref, head_ref, bias_ref, a_hbm, b_hbm, wide, narrow, tail, isem, osem, tsem):
    copies = []
    for k, (lo, n) in enumerate(CHUNKS):
        c = pltpu.make_async_copy(conv_hbm.at[pl.ds(lo, n)], wide.at[pl.ds(lo, n)], isem.at[k])
        c.start()
        copies.append(c)
    tail[...] = jnp.zeros_like(tail)
    tail[0:128, :] = stem_ref[...].astype(bf16)
    tail[128:144, :] = head_ref[...].astype(bf16)
    tail[144:147, :] = bias_ref[...].astype(bf16)
    last = pltpu.make_async_copy(tail, b_hbm.at[pl.ds(4608 - ROWS_A, 160)], tsem)
    last.start()
    outs = [last]
    for k, (lo, n) in enumerate(CHUNKS):
        copies[k].wait()

        @pl.loop(lo // 128, (lo + n) // 128)
        def _(q):
            r = pl.ds(pl.multiple_of(q * 128, 128), 128)
            narrow[r, :] = wide[r, :].astype(bf16)

        dst = a_hbm.at[pl.ds(lo, n)] if lo < ROWS_A else b_hbm.at[pl.ds(lo - ROWS_A, n)]
        c = pltpu.make_async_copy(narrow.at[pl.ds(lo, n)], dst, osem.at[k])
        c.start()
        outs.append(c)
    for c in outs:
        c.wait()


def pack(conv, stem, head, bias):
    vm = pl.BlockSpec(memory_space=pltpu.VMEM)
    hb = pl.BlockSpec(memory_space=pl.ANY)
    S = jax.ShapeDtypeStruct
    return pl.pallas_call(
        pack_kernel,
        out_shape=(S((ROWS_A, 256), bf16), S((ROWS_B, 256), bf16)),
        in_specs=[hb, vm, vm, vm],
        out_specs=(hb, hb),
        scratch_shapes=[
            pltpu.VMEM((4608, 256), f32),
            pltpu.VMEM((4608, 256), bf16),
            pltpu.VMEM((160, 256), bf16),
            pltpu.SemaphoreType.DMA((5,)),
            pltpu.SemaphoreType.DMA((5,)),
            pltpu.SemaphoreType.DMA,
        ],
        compiler_params=pltpu.CompilerParams(vmem_limit_bytes=16 * 1024 * 1024),
        cost_estimate=pl.CostEstimate(flops=1000000, bytes_accessed=7000000, transcendentals=0),
    )(conv, stem, head, bias)


FCH = 256


def mix_kernel(a_hbm, b_hbm, base_hbm, bstem_ref, bhead_ref, bbias_ref, new_hbm, nstem_ref, nhead_ref, nbias_ref,
               theirs, wide, asem, bsem, osem, tsem):
    n = 4608 // FCH
    tail = pltpu.make_async_copy(b_hbm.at[pl.ds(4608 - ROWS_A, 160)], theirs.at[pl.ds(4608, 160)], tsem)
    tail.start()
    for k in range(n):
        lo = k * FCH
        src = a_hbm.at[pl.ds(lo, FCH)] if lo < ROWS_A else b_hbm.at[pl.ds(lo - ROWS_A, FCH)]
        pltpu.make_async_copy(src, theirs.at[pl.ds(lo, FCH)], asem.at[k]).start()
        pltpu.make_async_copy(base_hbm.at[pl.ds(lo, FCH)], wide.at[pl.ds(lo, FCH)], bsem.at[k]).start()
    tail.wait()
    nstem_ref[...] = bstem_ref[...] + 0.5 * theirs[4608:4736, :].astype(f32)
    nhead_ref[...] = bhead_ref[...] + 0.5 * theirs[4736:4752, :].astype(f32)
    nbias_ref[...] = bbias_ref[...] + 0.5 * theirs[4752:4768, :].astype(f32)[0:3, :]
    for k in range(n):
        lo = k * FCH
        src = a_hbm.at[pl.ds(lo, FCH)] if lo < ROWS_A else b_hbm.at[pl.ds(lo - ROWS_A, FCH)]
        pltpu.make_async_copy(src, theirs.at[pl.ds(lo, FCH)], asem.at[k]).wait()
        pltpu.make_async_copy(base_hbm.at[pl.ds(lo, FCH)], wide.at[pl.ds(lo, FCH)], bsem.at[k]).wait()

        @pl.loop(lo // 128, (lo + FCH) // 128)
        def _(q):
            r = pl.ds(pl.multiple_of(q * 128, 128), 128)
            wide[r, :] = wide[r, :] + 0.5 * theirs[r, :].astype(f32)

        pltpu.make_async_copy(wide.at[pl.ds(lo, FCH)], new_hbm.at[pl.ds(lo, FCH)], osem.at[k]).start()
    for k in range(n):
        lo = k * FCH
        pltpu.make_async_copy(wide.at[pl.ds(lo, FCH)], new_hbm.at[pl.ds(lo, FCH)], osem.at[k]).wait()


def mix(a, b, base, bstem, bhead, bbias):
    vm = pl.BlockSpec(memory_space=pltpu.VMEM)
    hb = pl.BlockSpec(memory_space=pl.ANY)
    S = jax.ShapeDtypeStruct
    n = 4608 // FCH
    return pl.pallas_call(
        mix_kernel,
        out_shape=(S((4608, 256), f32), S((128, 256), f32), S((16, 256), f32), S((3, 256), f32)),
        in_specs=[hb, hb, hb, vm, vm, vm],
        out_specs=(hb, vm, vm, vm),
        scratch_shapes=[
            pltpu.VMEM((PACKED, 256), bf16),
            pltpu.VMEM((4608, 256), f32),
            pltpu.SemaphoreType.DMA((n,)),
            pltpu.SemaphoreType.DMA((n,)),
            pltpu.SemaphoreType.DMA((n,)),
            pltpu.SemaphoreType.DMA,
        ],
        compiler_params=pltpu.CompilerParams(vmem_limit_bytes=16 * 1024 * 1024),
        cost_estimate=pl.CostEstimate(flops=1000000, bytes_accessed=12000000, transcendentals=0),
    )(a, b, base, bstem, bhead, bbias)


def swap(array, bit):
    return lax.ppermute(array, BOTH, [(i, i ^ (1 << bit)) for i in range(256)])


def along_z(array, mask):
    return lax.ppermute(array, "dev", [(i, i ^ (mask << 1)) for i in range(32)])


COLUMNS = [[y * 8 + z * 2 + c for y in range(4) for c in range(2)] for z in range(4)]


def across(array):
    return lax.all_to_all(array, "dev", split_axis=0, concat_axis=0, axis_index_groups=COLUMNS, tiled=True)


def hold(first, *rest):
    return lax.optimization_barrier((first, *rest))


def step(bit, maps, heat, home, requests, counts, stem, conv, head, bias):
    mine = jnp.concatenate([maps.reshape(8, 8192), heat], axis=1)
    zpos = ((lax.axis_index("dev") >> 1) & 3).astype(jnp.int32).reshape(1)
    asked, sel = route(counts, zpos, requests.reshape(32, 1), home)
    wa, wb = pack(conv, stem, head, bias)
    if bit in (1,):
        others = [along_z(mine, m) for m in (1, 2, 3)]
        wa_out = None
    else:
        ta = swap(wa, bit)
        tb = None
        if bit not in (3, 4):
            tb = swap(wb, bit)
        others = [along_z(mine, m) for m in (1, 2, 3)]
    table = across(asked)
    if bit in (1,):
        wa2, wb2, *others = hold(wa, wb, *others)
        ta = swap(wa2, bit)
        tb = swap(wb2, bit)
    pick = (table.reshape(64, 1) == jnp.arange(32, dtype=jnp.int32)[None, :]).astype(bf16)
    pile = jnp.concatenate([mine, *others], axis=0)
    send = jnp.dot(pick, pile, preferred_element_type=f32).astype(bf16)
    got = across(send)
    if tb is None:
        wb2, got = hold(wb, got)
        tb = swap(wb2, bit)
    scale = 2.0 / (counts.astype(f32) * 1024.0)
    gconv, base, gstem, ghead, gbias, bstem, bhead, bbias = main_call(
        counts, scale, sel, got, wa, wb, bias, conv, stem, head
    )
    new, nstem, nhead, nbias = mix(ta, tb, base.reshape(4608, 256), bstem, bhead, bbias)
    return nstem, new, nhead, nbias, gstem, gconv, ghead, gbias


def local(step_number, maps, heat, home, requests, counts, stem, conv, head, bias):
    args = (maps, heat, home, requests, counts, stem[0], conv.reshape(4608, 256), head[0], bias[0])
    outs = lax.switch(step_number % 8, [functools.partial(step, bit) for bit in range(8)], *args)
    nstem, new, nhead, nbias, gstem, gconv, ghead, gbias = outs
    return (
        nstem[None], new.reshape(1, 2, 2304, 256), nhead[None], nbias[None],
        gstem[None], gconv.reshape(1, 2, 2304, 256), ghead[None], gbias[None],
    )


def solution(mesh):
    both = ("grp", "dev")
    placed = (
        P(),
        P(both, None, None),
        P(both, None),
        P("grp", None),
        P(both, None),
        P(both),
        P(both, None, None),
        P(both, None, None, None),
        P(both, None, None),
        P(both, None, None),
    )
    outs = (
        P(both, None, None),
        P(both, None, None, None),
        P(both, None, None),
        P(both, None, None),
        P(both, None, None),
        P(both, None, None, None),
        P(both, None, None),
        P(both, None, None),
    )
    return jax.shard_map(local, mesh=mesh, in_specs=placed, out_specs=outs, check_vma=False)
```

```python
import functools

import jax
import jax.numpy as jnp
from jax import lax
from jax.experimental import pallas as pl
from jax.experimental.pallas import tpu as pltpu
from jax.sharding import PartitionSpec as P

bf16 = jnp.bfloat16
f32 = jnp.float32
NT = (((1,), (1,)), ((), ()))
TN = (((0,), (0,)), ((), ()))
ROW_STEM = 4608
ROW_HEAD = 4736
PACKED = 4768


def dot(a, b):
    return jnp.dot(a, b, preferred_element_type=f32)


def block(i, n):
    return pl.ds(pl.multiple_of(i * n, n), n)


def main_kernel(
    count_ref, scale_ref, slot_ref, sel_ref, got_ref, w_hbm, bias_ref, conv_hbm, stem_ref, head_ref,
    gconv_hbm, base_hbm, gstem_ref, ghead_ref, gbias_ref, bstem_ref, bhead_ref, bbias_ref,
    wb, mine, gb, x_s, heat_s, act, act_t, grad, whe, err_s, err_t, bsum, gstem_acc,
    wsem, msem, osem, gsem, *, U, UB):
    wcopies = []
    for k, (lo, n) in enumerate(((ROW_STEM, PACKED - ROW_STEM), (0, ROW_STEM))):
        c = pltpu.make_async_copy(w_hbm.at[slot_ref[0], pl.ds(lo, n)], wb.at[pl.ds(lo, n)], wsem.at[k])
        c.start()
        wcopies.append(c)
    load_mine = pltpu.make_async_copy(conv_hbm, mine, msem)
    load_mine.start()

    edge = jnp.zeros((32, 256), bf16)

    @pl.loop(0, 10)
    def _(q):
        for buf, ks in ((act, (0, 1)), (grad, (1, 2))):
            for k in ks:
                buf[k, 0, block(q, 32), :] = edge
                buf[k, 9, block(q, 32), :] = edge
                buf[k, q, 0:32, :] = edge
                buf[k, q, 288:320, :] = edge

    sel = sel_ref[...]
    wcopies[0].wait()
    ws = wb[ROW_STEM:ROW_STEM + 128, :]
    b0 = bias_ref[0:1, :]

    @pl.loop(0, 8)
    def _(u):
        r = dot(sel, got_ref[:, block(u, 1024)]).astype(bf16)
        x = jnp.concatenate([r[:, v * 128:(v + 1) * 128] for v in range(8)], axis=0)
        x_s[u] = x
        heat_s[block(u, 32), :] = dot(sel, got_ref[:, pl.ds(pl.multiple_of(8192 + u * 128, 128), 128)])
        pre = dot(x, ws) + b0
        a = jnp.maximum(pre, 0.0).astype(bf16)
        act[0, u + 1, 32:288, :] = a
        act_t[0, :, block(u, 256)] = a.T

    wcopies[1].wait()
    n = 8 // U

    @pl.loop(0, 2 * n)
    def _(k):
        s = k // n
        u = (k - s * n) * U
        rows = []
        for e in range(U):
            rows.append(jnp.concatenate(
                [act[s, u + e + i, j * 32:j * 32 + 256, :] for i in range(3) for j in range(3)], axis=1))
        lhs = rows[0] if U == 1 else jnp.concatenate(rows, axis=0)
        pre = dot(lhs, wb[block(s, 2304), :]) + bias_ref[pl.ds(s + 1, 1), :]
        keep = s.astype(f32)
        for e in range(U):
            p = pre[e * 256:(e + 1) * 256] + keep * act[0, u + e + 1, 32:288, :].astype(f32)
            a = jnp.maximum(p, 0.0).astype(bf16)
            act[s + 1, u + e + 1, 32:288, :] = a
            act_t[s + 1, :, block(u + e, 256)] = a.T

    count = count_ref[0]
    scale = scale_ref[0]
    wh = wb[ROW_HEAD:ROW_HEAD + 16, :]

    def predict(v, pred):
        whe[v] = jnp.zeros((128, 256), bf16)
        whe[v, block(v, 16), :] = wh
        a = act[2, 1:9, pl.ds(pl.multiple_of(v * 32 + 32, 32), 32), :].reshape(256, 256)
        return pred + lax.dot_general(a, whe[v], NT, preferred_element_type=f32)

    pred = lax.fori_loop(0, 8, predict, jnp.zeros((256, 128), f32))
    row = lax.broadcasted_iota(jnp.int32, (256, 128), 0)
    err = jnp.where((row & 31) < count, (pred - heat_s[...]) * scale, 0.0).astype(bf16)
    err_s[...] = err
    err_t[...] = err.T
    bsum[...] = jnp.zeros_like(bsum)

    def spread(v, gh):
        at = pl.ds(pl.multiple_of(v * 32 + 32, 32), 32)
        a = act[2, 1:9, at, :].reshape(256, 256)
        d = jnp.where(a > 0, dot(err_s[...], whe[v]), 0.0).astype(bf16)
        bsum[2:3, :] += jnp.sum(d.astype(f32), axis=0, keepdims=True)
        grad[2, 1:9, at, :] = d.reshape(8, 32, 256)
        return gh + dot(err_t[block(v, 16), :], a)

    gh = lax.fori_loop(0, 8, spread, jnp.zeros((16, 256), f32))
    ghead_ref[...] = gh.astype(bf16)
    bhead_ref[...] = 0.5 * head_ref[...] - 0.1 * gh

    m = 8 // UB

    @pl.loop(0, 2 * m)
    def _(k):
        q = k // m
        s = 1 - q
        u = (k - q * m) * UB
        da = None
        for i in range(3):
            for j in range(3):
                ii, jj = 2 - i, 2 - j
                rows = [grad[s + 1, u + e + ii, jj * 32:jj * 32 + 256, :] for e in range(UB)]
                lhs = rows[0] if UB == 1 else jnp.concatenate(rows, axis=0)
                w = wb[pl.ds(pl.multiple_of(s * 2304 + (3 * i + j) * 256, 256), 256), :]
                t = lax.dot_general(lhs, w, NT, preferred_element_type=f32)
                da = t if da is None else da + t
        keep = q.astype(f32)
        for e in range(UB):
            d = da[e * 256:(e + 1) * 256] + keep * grad[2, u + e + 1, 32:288, :].astype(f32)
            d = jnp.where(act[s, u + e + 1, 32:288, :] > 0, d, 0.0).astype(bf16)
            grad[s, u + e + 1, 32:288, :] = d
            bsum[pl.ds(s, 1), :] += jnp.sum(d.astype(f32), axis=0, keepdims=True)

    gbias_ref[...] = bsum[0:3, :].astype(bf16)
    bbias_ref[...] = 0.5 * bias_ref[...] - 0.1 * bsum[0:3, :]
    gstem_acc[...] = jnp.zeros_like(gstem_acc)

    @pl.loop(0, 8)
    def _(u):
        gstem_acc[...] += lax.dot_general(x_s[u], grad[0, u + 1, 32:288, :], TN, preferred_element_type=f32)

    gs = gstem_acc[...]
    gstem_ref[...] = gs.astype(bf16)
    bstem_ref[...] = 0.5 * stem_ref[...] - 0.1 * gs

    load_mine.wait()

    def outs(t):
        r = block(t, 256)
        return (pltpu.make_async_copy(gb.at[r], gconv_hbm.at[r], gsem.at[t]),
                pltpu.make_async_copy(mine.at[r], base_hbm.at[r], osem.at[t]))

    @pl.loop(0, 18)
    def _(t):
        s = t // 9
        tap = t - s * 9
        ii = 2 - tap // 3
        jj = 2 - tap % 3
        rhs = jnp.concatenate([grad[s + 1, u + ii, pl.ds(pl.multiple_of(jj * 32, 32), 256), :] for u in range(8)], axis=0)
        g = dot(act_t[s], rhs)
        r = block(t, 256)
        gb[r, :] = g.astype(bf16)
        mine[r, :] = 0.5 * mine[r, :] - 0.1 * g
        for c in outs(t):
            c.start()

    @pl.loop(0, 18)
    def _(t):
        for c in outs(t):
            c.wait()


def main_call(count, scale, slot, sel, got, packed, bias, conv, stem, head, U=2, UB=2):
    vm = pl.BlockSpec(memory_space=pltpu.VMEM)
    sm = pl.BlockSpec(memory_space=pltpu.SMEM)
    hb = pl.BlockSpec(memory_space=pltpu.HBM)
    S = jax.ShapeDtypeStruct
    maps = pltpu.VMEM((3, 10, 320, 256), bf16)
    return pl.pallas_call(
        functools.partial(main_kernel, U=U, UB=UB),
        out_shape=(S((4608, 256), bf16), S((4608, 256), f32), S((128, 256), bf16), S((16, 256), bf16), S((3, 256), bf16),
                   S((128, 256), f32), S((16, 256), f32), S((3, 256), f32)),
        in_specs=[sm, sm, sm, vm, vm, hb, vm, hb, vm, vm],
        out_specs=(hb, hb, vm, vm, vm, vm, vm, vm),
        scratch_shapes=[
            pltpu.VMEM((PACKED, 256), bf16), pltpu.VMEM((4608, 256), f32), pltpu.VMEM((4608, 256), bf16),
            pltpu.VMEM((8, 256, 128), bf16), pltpu.VMEM((256, 128), f32), maps, pltpu.VMEM((3, 256, 2048), bf16), maps,
            pltpu.VMEM((8, 128, 256), bf16), pltpu.VMEM((256, 128), bf16), pltpu.VMEM((128, 256), bf16),
            pltpu.VMEM((8, 256), f32), pltpu.VMEM((128, 256), f32),
            pltpu.SemaphoreType.DMA((2,)), pltpu.SemaphoreType.DMA, pltpu.SemaphoreType.DMA((18,)), pltpu.SemaphoreType.DMA((18,)),
        ],
        compiler_params=pltpu.CompilerParams(vmem_limit_bytes=48 * 1024 * 1024),
        cost_estimate=pl.CostEstimate(flops=16_000_000_000, bytes_accessed=16_000_000, transcendentals=0),
    )(count, scale, slot, sel, got, packed, bias, conv, stem, head)


BOTH = ("grp", "dev")
COLUMNS = [[y * 8 + z * 2 + c for y in range(4) for c in range(2)] for z in range(4)]
ALONG_Z = [[y * 8 + z * 2 + c for z in range(4)] for y in range(4) for c in range(2)]


def prep_kernel(count_ref, req_ref, home_ref, maps_ref, heat_ref, asked_ref, sel_ref, mine_ref, wide):
    count = count_ref[0]
    wide[...] = maps_ref[...].reshape(512, 128).astype(f32)

    for p in range(64):
        mine_ref[0, :, p * 128:(p + 1) * 128] = wide[pl.ds(p, 8, stride=64), :].astype(bf16)
    mine_ref[0, :, 8192:9216] = heat_ref[...]
    for k in range(1, 4):
        mine_ref[k] = mine_ref[0]

    i = lax.broadcasted_iota(jnp.int32, (32, 32), 0)
    j = lax.broadcasted_iota(jnp.int32, (32, 32), 1)
    req = jnp.sum(jnp.where(i == j, req_ref[...], 0), axis=1, keepdims=True)
    lane = lax.broadcasted_iota(jnp.int32, (32, 256), 1)
    pos = jnp.sum(jnp.where(lane == req, home_ref[...], 0), axis=1, keepdims=True)
    owner = pos >> 3
    column = (owner >> 3) * 2 + (owner & 1)
    row = ((owner >> 1) & 3) * 8 + (pos & 7)
    across_lanes = jnp.sum(jnp.where(i == j, column, 0), axis=0, keepdims=True)
    live = lax.broadcasted_iota(jnp.int32, (32, 1), 0) < count
    earlier = (across_lanes == column) & (j < i) & (j < count)
    rank = jnp.minimum(jnp.sum(jnp.where(earlier, 1, 0), axis=1, keepdims=True), 7)
    lane64 = lax.broadcasted_iota(jnp.int32, (32, 64), 1)
    pick = jnp.where((lane64 == column * 8 + rank) & live, 1.0, 0.0)
    sel_ref[...] = pick.astype(bf16)
    value = jnp.broadcast_to((row + 1).astype(f32), (32, 128)).astype(bf16)
    asked = lax.dot_general(pick.astype(bf16), value, TN, preferred_element_type=f32)
    asked_ref[...] = (asked.astype(jnp.int32) - 1).reshape(8, 8, 128)


def prep(count, req, home, maps, heat):
    vm = pl.BlockSpec(memory_space=pltpu.VMEM)
    sm = pl.BlockSpec(memory_space=pltpu.SMEM)
    S = jax.ShapeDtypeStruct
    return pl.pallas_call(
        prep_kernel,
        out_shape=(S((8, 8, 128), jnp.int32), S((32, 64), bf16), S((4, 8, 9216), bf16)),
        in_specs=[sm, vm, vm, vm, vm],
        out_specs=(vm, vm, vm),
        scratch_shapes=[pltpu.VMEM((512, 128), f32)],
        compiler_params=pltpu.CompilerParams(vmem_limit_bytes=8 * 1024 * 1024),
    )(count, req, home, maps, heat)


def choose_kernel(table_ref, pile_ref, out_ref):
    lane = lax.broadcasted_iota(jnp.int32, (64, 32), 1)
    pick = jnp.where(table_ref[:, 0:32] == lane, 1.0, 0.0).astype(bf16)

    @pl.loop(0, 9)
    def _(k):
        out_ref[:, block(k, 1024)] = dot(pick, pile_ref[:, block(k, 1024)]).astype(bf16)


def choose(table, pile):
    vm = pl.BlockSpec(memory_space=pltpu.VMEM)
    return pl.pallas_call(
        choose_kernel,
        out_shape=jax.ShapeDtypeStruct((64, 9216), bf16),
        in_specs=[vm, vm],
        out_specs=vm,
        compiler_params=pltpu.CompilerParams(vmem_limit_bytes=8 * 1024 * 1024),
        cost_estimate=pl.CostEstimate(flops=40000000, bytes_accessed=2000000, transcendentals=0),
    )(table, pile)


PARTS = 4
PART = 4608 // PARTS


def pack_kernel(slot_ref, conv_hbm, stem_ref, head_ref, bias_ref, out_hbm, wide, narrow, isem, osem):
    def load(k):
        r = block(k, PART)
        return pltpu.make_async_copy(conv_hbm.at[r], wide.at[r], isem.at[k])

    def save(k):
        r = block(k, PART)
        return pltpu.make_async_copy(narrow.at[r], out_hbm.at[slot_ref[0], r], osem.at[k])

    for k in range(PARTS):
        load(k).start()
    narrow[4608:4736, :] = stem_ref[...].astype(bf16)
    narrow[4736:4752, :] = head_ref[...].astype(bf16)
    narrow[4752:4768, :] = jnp.concatenate([bias_ref[...], jnp.zeros((13, 256), f32)], axis=0).astype(bf16)
    last = pltpu.make_async_copy(
        narrow.at[pl.ds(4608, 160)], out_hbm.at[slot_ref[0], pl.ds(4608, 160)], osem.at[PARTS])
    last.start()

    @pl.loop(0, PARTS)
    def _(k):
        load(k).wait()

        @pl.loop(0, PART // 64)
        def _(q):
            r = pl.ds(pl.multiple_of(k * PART + q * 64, 64), 64)
            narrow[r, :] = wide[r, :].astype(bf16)

        save(k).start()

    for k in range(PARTS):
        save(k).wait()
    last.wait()


def pack(slot, conv, stem, head, bias):
    vm = pl.BlockSpec(memory_space=pltpu.VMEM)
    sm = pl.BlockSpec(memory_space=pltpu.SMEM)
    hb = pl.BlockSpec(memory_space=pltpu.HBM)
    return pl.pallas_call(
        pack_kernel,
        out_shape=jax.ShapeDtypeStruct((2, PACKED, 256), bf16),
        in_specs=[sm, hb, vm, vm, vm],
        out_specs=hb,
        scratch_shapes=[
            pltpu.VMEM((4608, 256), f32),
            pltpu.VMEM((PACKED, 256), bf16),
            pltpu.SemaphoreType.DMA((PARTS,)),
            pltpu.SemaphoreType.DMA((PARTS + 1,)),
        ],
        compiler_params=pltpu.CompilerParams(vmem_limit_bytes=16 * 1024 * 1024),
        cost_estimate=pl.CostEstimate(flops=1000000, bytes_accessed=7000000, transcendentals=0),
    )(slot, conv, stem, head, bias)


MIX = 8
PIECE = 4608 // MIX


def mix_kernel(slot_ref, t_hbm, base_hbm, bstem_ref, bhead_ref, bbias_ref, new_hbm, nstem_ref, nhead_ref, nbias_ref,
               theirs, wide, asem, bsem, osem):
    def loads(k):
        r = block(k, PIECE)
        return (pltpu.make_async_copy(t_hbm.at[slot_ref[0], r], theirs.at[r], asem.at[k]),
                pltpu.make_async_copy(base_hbm.at[r], wide.at[r], bsem.at[k]))

    def save(k):
        r = block(k, PIECE)
        return pltpu.make_async_copy(wide.at[r], new_hbm.at[r], osem.at[k])

    tail = pltpu.make_async_copy(t_hbm.at[slot_ref[0], pl.ds(4608, 160)], theirs.at[pl.ds(4608, 160)], asem.at[MIX])
    for k in range(MIX):
        for c in loads(k):
            c.start()
    tail.start()

    @pl.loop(0, MIX)
    def _(k):
        for c in loads(k):
            c.wait()

        @pl.loop(0, PIECE // 64)
        def _(q):
            r = pl.ds(pl.multiple_of(k * PIECE + q * 64, 64), 64)
            wide[r, :] = wide[r, :] + 0.5 * theirs[r, :].astype(f32)

        save(k).start()

    tail.wait()
    nstem_ref[...] = bstem_ref[...] + 0.5 * theirs[4608:4736, :].astype(f32)
    nhead_ref[...] = bhead_ref[...] + 0.5 * theirs[4736:4752, :].astype(f32)
    nbias_ref[...] = bbias_ref[...] + 0.5 * theirs[4752:4768, :].astype(f32)[0:3, :]
    for k in range(MIX):
        save(k).wait()


def mix(slot, theirs, base, bstem, bhead, bbias):
    vm = pl.BlockSpec(memory_space=pltpu.VMEM)
    sm = pl.BlockSpec(memory_space=pltpu.SMEM)
    hb = pl.BlockSpec(memory_space=pltpu.HBM)
    S = jax.ShapeDtypeStruct
    return pl.pallas_call(
        mix_kernel,
        out_shape=(S((4608, 256), f32), S((128, 256), f32), S((16, 256), f32), S((3, 256), f32)),
        in_specs=[sm, hb, hb, vm, vm, vm],
        out_specs=(hb, vm, vm, vm),
        scratch_shapes=[
            pltpu.VMEM((PACKED, 256), bf16),
            pltpu.VMEM((4608, 256), f32),
            pltpu.SemaphoreType.DMA((MIX + 1,)),
            pltpu.SemaphoreType.DMA((MIX,)),
            pltpu.SemaphoreType.DMA((MIX,)),
        ],
        compiler_params=pltpu.CompilerParams(vmem_limit_bytes=16 * 1024 * 1024),
        cost_estimate=pl.CostEstimate(flops=1000000, bytes_accessed=12000000, transcendentals=0),
    )(slot, theirs, base, bstem, bhead, bbias)


def swap(array, bit):
    pairs = [[i, i ^ (1 << bit)] for i in range(256) if not i >> bit & 1]
    return lax.all_to_all(array, BOTH, split_axis=0, concat_axis=0, axis_index_groups=pairs, tiled=True)


def among(array, groups):
    return lax.all_to_all(array, "dev", split_axis=0, concat_axis=0, axis_index_groups=groups, tiled=True)


def step(bit, counts, scale, slot, asked, sel, mine, packed, bias, conv, stem, head):
    if bit != 1:
        theirs = swap(packed, bit)
    pile = among(mine, ALONG_Z)
    table = among(asked, COLUMNS)
    if bit == 1:
        packed_late, pile, table = lax.optimization_barrier((packed, pile, table))
        theirs = swap(packed_late, bit)
    send = choose(table.reshape(64, 128), pile.reshape(32, 9216))
    got = among(send.reshape(8, 8, 9216), COLUMNS)
    outs = main_call(counts, scale, slot, sel, got.reshape(64, 9216), packed, bias, conv, stem, head)
    return (theirs, *outs)


def local(step_number, maps, heat, home, requests, counts, stem, conv, head, bias):
    bit = step_number % 8
    stem, conv, head, bias = stem[0], conv.reshape(4608, 256), head[0], bias[0]
    me = lax.axis_index("grp") * 32 + lax.axis_index("dev")
    slot = (1 - ((me >> bit) & 1)).astype(jnp.int32).reshape(1)
    scale = 2.0 / (counts.astype(f32) * 1024.0)
    packed = pack(slot, conv, stem, head, bias)
    asked, sel, mine = prep(counts, requests, home, maps, heat)
    outs = lax.switch(
        bit, [functools.partial(step, b) for b in range(8)],
        counts, scale, slot, asked, sel, mine, packed, bias, conv, stem, head,
    )
    theirs, gconv, base, gstem, ghead, gbias, bstem, bhead, bbias = outs
    new, nstem, nhead, nbias = mix(slot, theirs, base, bstem, bhead, bbias)
    return (
        nstem[None], new.reshape(1, 2, 2304, 256), nhead[None], nbias[None],
        gstem[None], gconv.reshape(1, 2, 2304, 256), ghead[None], gbias[None],
    )


def solution(mesh):
    placed = (
        P(),
        P(BOTH, None, None),
        P(BOTH, None),
        P("grp", None),
        P(BOTH, None),
        P(BOTH),
        P(BOTH, None, None),
        P(BOTH, None, None, None),
        P(BOTH, None, None),
        P(BOTH, None, None),
    )
    outs = (
        P(BOTH, None, None),
        P(BOTH, None, None, None),
        P(BOTH, None, None),
        P(BOTH, None, None),
        P(BOTH, None, None),
        P(BOTH, None, None, None),
        P(BOTH, None, None),
        P(BOTH, None, None),
    )
    return jax.shard_map(local, mesh=mesh, in_specs=placed, out_specs=outs, check_vma=False)
```

```python
import functools

import jax
import jax.numpy as jnp
from jax import lax
from jax.experimental import pallas as pl
from jax.experimental.pallas import tpu as pltpu
from jax.sharding import PartitionSpec as P


bf16 = jnp.bfloat16
f32 = jnp.float32
NT = (((1,), (1,)), ((), ()))
TN = (((0,), (0,)), ((), ()))
ROW_STEM = 4608
ROW_HEAD = 4736
PACKED = 4768


def dot(a, b):
    return jnp.dot(a, b, preferred_element_type=f32)


def block(i, n):
    return pl.ds(pl.multiple_of(i * n, n), n)


def main_kernel(
    count_ref, scale_ref, sel_ref, got_ref, w_hbm, bias_ref, conv_hbm, stem_ref, head_ref,
    gconv_hbm, base_hbm, gstem_ref, ghead_ref, gbias_ref,
    wb, mine, gb, x_s, heat_s, act, act_t, grad, whe, err_s, err_t, bsum, gstem_acc,
    tail, wsem, msem, tsem, osem, gsem, *, U, UB):
    wcopies = []
    for k, (lo, n) in enumerate(((ROW_STEM, PACKED - ROW_STEM), (0, ROW_STEM))):
        c = pltpu.make_async_copy(w_hbm.at[pl.ds(lo, n)], wb.at[pl.ds(lo, n)], wsem.at[k])
        c.start()
        wcopies.append(c)
    load_mine = pltpu.make_async_copy(conv_hbm, mine, msem)
    load_mine.start()

    edge = jnp.zeros((32, 256), bf16)

    @pl.loop(0, 10)
    def _(q):
        for buf, ks in ((act, (0, 1)), (grad, (1, 2))):
            for k in ks:
                buf[k, 0, block(q, 32), :] = edge
                buf[k, 9, block(q, 32), :] = edge
                buf[k, q, 0:32, :] = edge
                buf[k, q, 288:320, :] = edge

    @pl.loop(0, 6)
    def _(q):
        z = jnp.zeros((256, 256), bf16)
        act_t[q // 3, q % 3, :, 0:256] = z
        act_t[q // 3, q % 3, :, 2304:2560] = z

    sel = sel_ref[...]
    wcopies[0].wait()
    ws = wb[ROW_STEM:ROW_STEM + 128, :]
    b0 = bias_ref[0]

    @pl.loop(0, 8)
    def _(u):
        r = dot(sel, got_ref[:, block(u, 1024)]).astype(bf16)
        x = jnp.concatenate([r[:, v * 128:(v + 1) * 128] for v in range(8)], axis=0)
        x_s[u] = x
        heat_s[block(u, 32), :] = dot(sel, got_ref[:, pl.ds(pl.multiple_of(8192 + u * 128, 128), 128)])
        pre = dot(x, ws) + b0
        a = jnp.maximum(pre, 0.0).astype(bf16)
        act[0, u + 1, 32:288, :] = a

    wcopies[1].wait()
    n = 8 // U

    @pl.loop(0, 2 * n)
    def _(k):
        s = k // n
        u = (k - s * n) * U
        rows = []
        for e in range(U):
            rows.append(jnp.concatenate(
                [act[s, u + e + i, j * 32:j * 32 + 256, :] for i in range(3) for j in range(3)], axis=1))
        lhs = rows[0] if U == 1 else jnp.concatenate(rows, axis=0)
        pre = dot(lhs, wb[block(s, 2304), :]) + bias_ref[s + 1]
        for e in range(U):
            for j in range(3):
                act_t[s, j, :, block(u + e + 1, 256)] = act[s, u + e + 1, j * 32:j * 32 + 256, :].T
        keep = s.astype(f32)
        for e in range(U):
            p = pre[e * 256:(e + 1) * 256] + keep * act[0, u + e + 1, 32:288, :].astype(f32)
            a = jnp.maximum(p, 0.0).astype(bf16)
            act[s + 1, u + e + 1, 32:288, :] = a

    count = count_ref[0]
    scale = scale_ref[0]
    wh = wb[ROW_HEAD:ROW_HEAD + 16, :]

    def predict(v, pred):
        whe[v] = jnp.zeros((128, 256), bf16)
        whe[v, block(v, 16), :] = wh
        a = act[2, 1:9, pl.ds(pl.multiple_of(v * 32 + 32, 32), 32), :].reshape(256, 256)
        return pred + lax.dot_general(a, whe[v], NT, preferred_element_type=f32)

    pred = lax.fori_loop(0, 8, predict, jnp.zeros((256, 128), f32))
    row = lax.broadcasted_iota(jnp.int32, (256, 128), 0)
    err = jnp.where((row & 31) < count, (pred - heat_s[...]) * scale, 0.0).astype(bf16)
    err_s[...] = err
    err_t[...] = err.T
    bsum[...] = jnp.zeros_like(bsum)

    def spread(v, gh):
        at = pl.ds(pl.multiple_of(v * 32 + 32, 32), 32)
        a = act[2, 1:9, at, :].reshape(256, 256)
        d = jnp.where(a > 0, dot(err_s[...], whe[v]), 0.0).astype(bf16)
        bsum[2:3, :] += jnp.sum(d.astype(f32), axis=0, keepdims=True)
        grad[2, 1:9, at, :] = d.reshape(8, 32, 256)
        return gh + dot(err_t[block(v, 16), :], a)

    gh = lax.fori_loop(0, 8, spread, jnp.zeros((16, 256), f32))
    ghead_ref[...] = gh.astype(bf16)
    tail[128:144, :] = 0.5 * head_ref[...] - 0.1 * gh

    m = 8 // UB

    @pl.loop(0, 2 * m)
    def _(k):
        q = k // m
        s = 1 - q
        u = (k - q * m) * UB
        da = None
        for i in range(3):
            for j in range(3):
                ii, jj = 2 - i, 2 - j
                rows = [grad[s + 1, u + e + ii, jj * 32:jj * 32 + 256, :] for e in range(UB)]
                lhs = rows[0] if UB == 1 else jnp.concatenate(rows, axis=0)
                w = wb[pl.ds(pl.multiple_of(s * 2304 + (3 * i + j) * 256, 256), 256), :]
                t = lax.dot_general(lhs, w, NT, preferred_element_type=f32)
                da = t if da is None else da + t
        keep = q.astype(f32)
        for e in range(UB):
            d = da[e * 256:(e + 1) * 256] + keep * grad[2, u + e + 1, 32:288, :].astype(f32)
            d = jnp.where(act[s, u + e + 1, 32:288, :] > 0, d, 0.0).astype(bf16)
            grad[s, u + e + 1, 32:288, :] = d
            bsum[pl.ds(s, 1), :] += jnp.sum(d.astype(f32), axis=0, keepdims=True)

    gbias_ref[...] = bsum[0:3, :].astype(bf16)
    tail[144:152, :] = 0.5 * jnp.concatenate([bias_ref[0], bias_ref[1], bias_ref[2], jnp.zeros((5, 256), f32)], axis=0) - 0.1 * bsum[...]
    tail[152:160, :] = jnp.zeros((8, 256), f32)
    gstem_acc[...] = jnp.zeros_like(gstem_acc)

    @pl.loop(0, 8)
    def _(u):
        gstem_acc[...] += lax.dot_general(x_s[u], grad[0, u + 1, 32:288, :], TN, preferred_element_type=f32)

    gs = gstem_acc[...]
    gstem_ref[...] = gs.astype(bf16)
    tail[0:128, :] = 0.5 * stem_ref[...] - 0.1 * gs
    save_tail = pltpu.make_async_copy(tail, base_hbm.at[pl.ds(ROW_STEM, 160)], tsem)
    save_tail.start()

    load_mine.wait()

    def outs(t):
        r = block(t, 256)
        return (pltpu.make_async_copy(gb.at[r], gconv_hbm.at[r], gsem.at[t]),
                pltpu.make_async_copy(mine.at[r], base_hbm.at[r], osem.at[t]))

    @pl.loop(0, 6)
    def _(q):
        s = q // 3
        j = q - s * 3
        rhs = grad[s + 1, 1:9, 32:288, :].reshape(2048, 256)
        lhs = jnp.concatenate([act_t[s, j, :, i * 256:i * 256 + 2048] for i in range(3)], axis=0)
        all_rows = dot(lhs, rhs)
        for i in range(3):
            t = s * 9 + i * 3 + j
            g = all_rows[i * 256:(i + 1) * 256]
            r = block(t, 256)
            gb[r, :] = g.astype(bf16)
            mine[r, :] = 0.5 * mine[r, :] - 0.1 * g
            for c in outs(t):
                c.start()

    @pl.loop(0, 18)
    def _(t):
        for c in outs(t):
            c.wait()

    save_tail.wait()


def main_call(count, scale, sel, got, packed, bias, conv, stem, head, U=4, UB=2):
    vm = pl.BlockSpec(memory_space=pltpu.VMEM)
    sm = pl.BlockSpec(memory_space=pltpu.SMEM)
    hb = pl.BlockSpec(memory_space=pltpu.HBM)
    S = jax.ShapeDtypeStruct
    maps = pltpu.VMEM((3, 10, 320, 256), bf16)
    return pl.pallas_call(
        functools.partial(main_kernel, U=U, UB=UB),
        out_shape=(S((4608, 256), bf16), S((PACKED, 256), f32), S((128, 256), bf16), S((16, 256), bf16), S((3, 256), bf16)),
        in_specs=[sm, sm, vm, vm, hb, vm, hb, vm, vm],
        out_specs=(hb, hb, vm, vm, vm),
        scratch_shapes=[
            pltpu.VMEM((PACKED, 256), bf16), pltpu.VMEM((4608, 256), f32), pltpu.VMEM((4608, 256), bf16),
            pltpu.VMEM((8, 256, 128), bf16), pltpu.VMEM((256, 128), f32), maps, pltpu.VMEM((2, 3, 256, 2560), bf16), maps,
            pltpu.VMEM((8, 128, 256), bf16), pltpu.VMEM((256, 128), bf16), pltpu.VMEM((128, 256), bf16),
            pltpu.VMEM((8, 256), f32), pltpu.VMEM((128, 256), f32), pltpu.VMEM((160, 256), f32),
            pltpu.SemaphoreType.DMA((2,)), pltpu.SemaphoreType.DMA, pltpu.SemaphoreType.DMA, pltpu.SemaphoreType.DMA((18,)), pltpu.SemaphoreType.DMA((18,)),
        ],
        compiler_params=pltpu.CompilerParams(vmem_limit_bytes=48 * 1024 * 1024),
        cost_estimate=pl.CostEstimate(flops=16_000_000_000, bytes_accessed=16_000_000, transcendentals=0),
    )(count, scale, sel, got, packed, bias, conv, stem, head)


BOTH = ("grp", "dev")
COLUMNS = [[y * 8 + z * 2 + c for y in range(4) for c in range(2)] for z in range(4)]


def prep_kernel(count_ref, zpos_ref, req_hbm, home_hbm, maps_hbm, heat_hbm, asked_ref, sel_ref, mine_ref, req, home, heat, maps, wide, sems):
    copies = [
        pltpu.make_async_copy(src, dst, sems.at[k])
        for k, (src, dst) in enumerate(((maps_hbm, maps), (heat_hbm, heat), (req_hbm, req), (home_hbm, home)))
    ]
    for c in copies:
        c.start()
    count = count_ref[0]
    copies[2].wait()
    copies[3].wait()
    i = lax.broadcasted_iota(jnp.int32, (32, 32), 0)
    j = lax.broadcasted_iota(jnp.int32, (32, 32), 1)
    wanted = jnp.sum(jnp.where(i == j, req[...], 0), axis=1, keepdims=True)
    lane = lax.broadcasted_iota(jnp.int32, (32, 256), 1)
    pos = jnp.sum(jnp.where(lane == wanted, home[...], 0), axis=1, keepdims=True)
    owner = pos >> 3
    column = (owner >> 3) * 2 + (owner & 1)
    row = (((owner >> 1) & 3) ^ zpos_ref[0]) * 8 + (pos & 7)
    across_lanes = jnp.sum(jnp.where(i == j, column, 0), axis=0, keepdims=True)
    live = lax.broadcasted_iota(jnp.int32, (32, 1), 0) < count
    earlier = (across_lanes == column) & (j < i) & (j < count)
    rank = jnp.minimum(jnp.sum(jnp.where(earlier, 1, 0), axis=1, keepdims=True), 7)
    lane64 = lax.broadcasted_iota(jnp.int32, (32, 64), 1)
    pick = jnp.where((lane64 == column * 8 + rank) & live, 1.0, 0.0)
    sel_ref[...] = pick.astype(bf16)
    value = jnp.broadcast_to((row + 1).astype(f32), (32, 128)).astype(bf16)
    asked = lax.dot_general(pick.astype(bf16), value, TN, preferred_element_type=f32)
    asked_ref[...] = (asked.astype(jnp.int32) - 1).reshape(8, 8, 128)
    copies[0].wait()
    wide[...] = maps[...].reshape(512, 128).astype(f32)
    for p in range(64):
        mine_ref[:, p * 128:(p + 1) * 128] = wide[pl.ds(p, 8, stride=64), :].astype(bf16)
    copies[1].wait()
    mine_ref[:, 8192:9216] = heat[...]


def prep(count, zpos, req, home, maps, heat):
    vm = pl.BlockSpec(memory_space=pltpu.VMEM)
    sm = pl.BlockSpec(memory_space=pltpu.SMEM)
    hb = pl.BlockSpec(memory_space=pltpu.HBM)
    S = jax.ShapeDtypeStruct
    return pl.pallas_call(
        prep_kernel,
        out_shape=(S((8, 8, 128), jnp.int32), S((32, 64), bf16), S((8, 9216), bf16)),
        in_specs=[sm, sm, hb, hb, hb, hb],
        out_specs=(vm, vm, vm),
        scratch_shapes=[
            pltpu.VMEM((1, 32), jnp.int32),
            pltpu.VMEM((1, 256), jnp.int32),
            pltpu.VMEM((8, 1024), bf16),
            pltpu.VMEM((8, 64, 128), bf16),
            pltpu.VMEM((512, 128), f32),
            pltpu.SemaphoreType.DMA((4,)),
        ],
        compiler_params=pltpu.CompilerParams(vmem_limit_bytes=60 * 1024 * 1024),
    )(count, zpos, req, home, maps, heat)


def choose_kernel(table_ref, *refs):
    *piles, out_ref = refs
    lane = lax.broadcasted_iota(jnp.int32, (64, 32), 1)
    pick = jnp.where(table_ref[:, 0:32] == lane, 1.0, 0.0).astype(bf16)

    @pl.loop(0, 9)
    def _(k):
        pile = jnp.concatenate([p[:, block(k, 1024)] for p in piles], axis=0)
        out_ref[:, block(k, 1024)] = dot(pick, pile).astype(bf16)


def choose(table, *piles):
    vm = pl.BlockSpec(memory_space=pltpu.VMEM)
    return pl.pallas_call(
        choose_kernel,
        out_shape=jax.ShapeDtypeStruct((64, 9216), bf16),
        in_specs=[vm] * 5,
        out_specs=vm,
        compiler_params=pltpu.CompilerParams(vmem_limit_bytes=8 * 1024 * 1024),
        cost_estimate=pl.CostEstimate(flops=40000000, bytes_accessed=2000000, transcendentals=0),
    )(table, *piles)


PARTS = 6
PART = 4608 // PARTS


def pack_kernel(conv_hbm, stem_hbm, head_hbm, bias_hbm, out_hbm, wide, bias, narrow, isem, osem):
    def load(k):
        r = block(k, PART)
        return pltpu.make_async_copy(conv_hbm.at[r], wide.at[r], isem.at[k])

    def save(k):
        r = block(k, PART)
        return pltpu.make_async_copy(narrow.at[r], out_hbm.at[r], osem.at[k])

    def save_tail():
        r = pl.ds(ROW_STEM, 160)
        return pltpu.make_async_copy(narrow.at[r], out_hbm.at[r], osem.at[PARTS])

    small = [
        pltpu.make_async_copy(stem_hbm, wide.at[pl.ds(ROW_STEM, 128)], isem.at[PARTS]),
        pltpu.make_async_copy(head_hbm, wide.at[pl.ds(ROW_HEAD, 16)], isem.at[PARTS + 1]),
        pltpu.make_async_copy(bias_hbm, bias, isem.at[PARTS + 2]),
    ]
    for k in range(PARTS):
        load(k).start()
    for c in small:
        c.start()

    def narrowed(lo, n):
        @pl.loop(0, n // 48)
        def _(q):
            r = pl.ds(pl.multiple_of(lo + q * 48, 16), 48)
            narrow[r, :] = wide[r, :].astype(bf16)

    @pl.loop(0, PARTS)
    def _(k):
        load(k).wait()
        narrowed(k * PART, PART)
        save(k).start()

    for c in small:
        c.wait()
    narrowed(ROW_STEM, 144)
    narrow[ROW_STEM + 144:PACKED, :] = jnp.concatenate([bias[0], bias[1], bias[2], jnp.zeros((13, 256), f32)], axis=0).astype(bf16)
    save_tail().start()

    @pl.loop(0, PARTS)
    def _(k):
        save(k).wait()

    save_tail().wait()


def pack(conv, stem, head, bias):
    hb = pl.BlockSpec(memory_space=pltpu.HBM)
    return pl.pallas_call(
        pack_kernel,
        out_shape=jax.ShapeDtypeStruct((PACKED, 256), bf16),
        in_specs=[hb, hb, hb, hb],
        out_specs=hb,
        scratch_shapes=[
            pltpu.VMEM((PACKED, 256), f32),
            pltpu.VMEM((3, 1, 256), f32),
            pltpu.VMEM((PACKED, 256), bf16),
            pltpu.SemaphoreType.DMA((PARTS + 3,)),
            pltpu.SemaphoreType.DMA((PARTS + 1,)),
        ],
        compiler_params=pltpu.CompilerParams(vmem_limit_bytes=16 * 1024 * 1024),
        cost_estimate=pl.CostEstimate(flops=1000000, bytes_accessed=7000000, transcendentals=0),
    )(conv, stem, head, bias)


MIX = 8
PIECE = 4608 // MIX


def mix_kernel(t_hbm, base_hbm, new_hbm, nstem_hbm, nhead_hbm, nbias_ref, theirs, wide, asem, bsem, osem):
    def loads(k, r):
        return (pltpu.make_async_copy(t_hbm.at[r], theirs.at[r], asem.at[k]),
                pltpu.make_async_copy(base_hbm.at[r], wide.at[r], bsem.at[k]))

    def save(k):
        r = block(k, PIECE)
        return pltpu.make_async_copy(wide.at[r], new_hbm.at[r], osem.at[k])

    last = loads(MIX, pl.ds(ROW_STEM, 160))
    for c in last:
        c.start()
    for k in range(MIX):
        for c in loads(k, block(k, PIECE)):
            c.start()

    def mixed(lo, n):
        @pl.loop(0, n // 32)
        def _(q):
            r = pl.ds(pl.multiple_of(lo + q * 32, 32), 32)
            wide[r, :] = wide[r, :] + 0.5 * theirs[r, :].astype(f32)

    for c in last:
        c.wait()
    mixed(ROW_STEM, 160)
    small = (pltpu.make_async_copy(wide.at[pl.ds(ROW_STEM, 128)], nstem_hbm, osem.at[MIX]),
             pltpu.make_async_copy(wide.at[pl.ds(ROW_HEAD, 16)], nhead_hbm, osem.at[MIX + 1]))
    for c in small:
        c.start()
    for k in range(3):
        nbias_ref[k] = wide[ROW_HEAD + 16 + k:ROW_HEAD + 17 + k, :]

    @pl.loop(0, MIX)
    def _(k):
        for c in loads(k, block(k, PIECE)):
            c.wait()
        mixed(k * PIECE, PIECE)
        save(k).start()

    @pl.loop(0, MIX)
    def _(k):
        save(k).wait()

    for c in small:
        c.wait()


def mix(theirs, base):
    vm = pl.BlockSpec(memory_space=pltpu.VMEM)
    hb = pl.BlockSpec(memory_space=pltpu.HBM)
    S = jax.ShapeDtypeStruct
    return pl.pallas_call(
        mix_kernel,
        out_shape=(S((4608, 256), f32), S((128, 256), f32), S((16, 256), f32), S((3, 1, 256), f32)),
        in_specs=[hb, hb],
        out_specs=(hb, hb, hb, vm),
        scratch_shapes=[
            pltpu.VMEM((PACKED, 256), bf16),
            pltpu.VMEM((PACKED, 256), f32),
            pltpu.SemaphoreType.DMA((MIX + 1,)),
            pltpu.SemaphoreType.DMA((MIX + 1,)),
            pltpu.SemaphoreType.DMA((MIX + 2,)),
        ],
        compiler_params=pltpu.CompilerParams(vmem_limit_bytes=16 * 1024 * 1024),
        cost_estimate=pl.CostEstimate(flops=1000000, bytes_accessed=12000000, transcendentals=0),
    )(theirs, base)


def swap(array, bit):
    return lax.ppermute(array, BOTH, [(i, i ^ (1 << bit)) for i in range(256)])


def along_z(array, mask):
    return lax.ppermute(array, "dev", [(i, i ^ (mask << 1)) for i in range(32)])


def among(array):
    return lax.all_to_all(array, "dev", split_axis=0, concat_axis=0, axis_index_groups=COLUMNS, tiled=True)


def step(bit, counts, scale, sel, send, packed, bias, conv, stem, head):
    theirs = swap(packed, bit)
    got = among(send)
    outs = main_call(counts, scale, sel, got.reshape(64, 9216), packed, bias, conv, stem, head)
    return (theirs, *outs)


def local(step_number, maps, heat, home, requests, counts, stem, conv, head, bias):
    stem, conv, head, bias = stem[0], conv.reshape(4608, 256), head[0], jnp.transpose(bias, (1, 0, 2))
    zpos = ((lax.axis_index("dev") >> 1) & 3).astype(jnp.int32).reshape(1)
    scale = 2.0 / (counts.astype(f32) * 1024.0)
    asked, sel, mine = prep(counts, zpos, requests, home, maps, heat)
    others = [along_z(mine, mask) for mask in (1, 2, 3)]
    table = among(asked)
    packed = pack(conv, stem, head, bias)
    send = choose(table.reshape(64, 128), mine, *others)
    outs = lax.switch(
        step_number % 8, [functools.partial(step, b) for b in range(8)],
        counts, scale, sel, send.reshape(8, 8, 9216), packed, bias, conv, stem, head,
    )
    theirs, gconv, base, gstem, ghead, gbias = outs
    new, nstem, nhead, nbias = mix(theirs, base)
    return (
        nstem[None], new.reshape(1, 2, 2304, 256), nhead[None], jnp.transpose(nbias, (1, 0, 2)),
        gstem[None], gconv.reshape(1, 2, 2304, 256), ghead[None], gbias[None],
    )


def solution(mesh):
    placed = (
        P(),
        P(BOTH, None, None),
        P(BOTH, None),
        P("grp", None),
        P(BOTH, None),
        P(BOTH),
        P(BOTH, None, None),
        P(BOTH, None, None, None),
        P(BOTH, None, None),
        P(BOTH, None, None),
    )
    outs = (
        P(BOTH, None, None),
        P(BOTH, None, None, None),
        P(BOTH, None, None),
        P(BOTH, None, None),
        P(BOTH, None, None),
        P(BOTH, None, None, None),
        P(BOTH, None, None),
        P(BOTH, None, None),
    )
    return jax.shard_map(local, mesh=mesh, in_specs=placed, out_specs=outs, check_vma=False)
```

```python
import functools

import jax
import jax.numpy as jnp
from jax import lax
from jax.experimental import pallas as pl
from jax.experimental.pallas import tpu as pltpu
from jax.sharding import PartitionSpec as P


bf16 = jnp.bfloat16
f32 = jnp.float32
NT = (((1,), (1,)), ((), ()))
TN = (((0,), (0,)), ((), ()))
ROW_STEM = 4608
ROW_HEAD = 4736
PACKED = 4768


def dot(a, b):
    return jnp.dot(a, b, preferred_element_type=f32)


def block(i, n):
    return pl.ds(pl.multiple_of(i * n, n), n)


def main_kernel(
    weight_ref, sel_ref, got_ref, w_hbm, bias_ref, conv_hbm, stem_ref, head_ref,
    gconv_hbm, base_hbm, gstem_ref, ghead_ref, gbias_ref,
    wb, mine, gb, x_t, heat_s, act, act_t, grad, whe, err_s, err_t, bsum,
    tail, wsem, msem, tsem, osem, gsem, *, U, UB, HU, HV, ONE):
    wcopies = []
    for k, (lo, n) in enumerate(((ROW_STEM, PACKED - ROW_STEM), (0, ROW_STEM))):
        c = pltpu.make_async_copy(w_hbm.at[pl.ds(lo, n)], wb.at[pl.ds(lo, n)], wsem.at[k])
        c.start()
        wcopies.append(c)
    load_mine = pltpu.make_async_copy(conv_hbm, mine, msem)

    edge = jnp.zeros((32, 256), bf16)

    @pl.loop(0, 10)
    def _(q):
        for buf, ks in ((act, (0, 1)), (grad, (1, 2))):
            for k in ks:
                buf[k, 0, block(q, 32), :] = edge
                buf[k, 9, block(q, 32), :] = edge
                buf[k, q, 0:32, :] = edge
                buf[k, q, 288:320, :] = edge

    @pl.loop(0, 6)
    def _(q):
        z = jnp.zeros((256, 256), bf16)
        act_t[q // 3, q % 3, :, 0:256] = z
        act_t[q // 3, q % 3, :, 2304:2560] = z

    sel = sel_ref[...]
    wcopies[0].wait()
    ws = wb[ROW_STEM:ROW_STEM + 128, :]
    b0 = bias_ref[0]

    @pl.loop(0, 8)
    def _(u):
        r = dot(sel, got_ref[:, block(u, 1024)]).astype(bf16)
        x = jnp.concatenate([r[:, v * 128:(v + 1) * 128] for v in range(8)], axis=0)
        x_t[:, block(u, 256)] = x.T
        heat_s[block(u, 32), :] = dot(sel, got_ref[:, pl.ds(pl.multiple_of(8192 + u * 128, 128), 128)])
        pre = dot(x, ws) + b0
        a = jnp.maximum(pre, 0.0).astype(bf16)
        act[0, u + 1, 32:288, :] = a

    wcopies[1].wait()
    load_mine.start()
    n = 8 // U

    @pl.loop(0, 2 * n)
    def _(k):
        s = k // n
        u = (k - s * n) * U
        rows = []
        for e in range(U):
            rows.append(jnp.concatenate(
                [act[s, u + e + i, j * 32:j * 32 + 256, :] for i in range(3) for j in range(3)], axis=1))
        lhs = rows[0] if U == 1 else jnp.concatenate(rows, axis=0)
        pre = dot(lhs, wb[block(s, 2304), :]) + bias_ref[s + 1]
        for e in range(U):
            for j in range(3):
                act_t[s, j, :, block(u + e + 1, 256)] = act[s, u + e + 1, j * 32:j * 32 + 256, :].T
        keep = s.astype(f32)
        for e in range(U):
            p = pre[e * 256:(e + 1) * 256] + keep * act[0, u + e + 1, 32:288, :].astype(f32)
            a = jnp.maximum(p, 0.0).astype(bf16)
            act[s + 1, u + e + 1, 32:288, :] = a

    wh = wb[ROW_HEAD:ROW_HEAD + 16, :]

    def predict(v, pred):
        whe[v] = jnp.zeros((128, 256), bf16)
        whe[v, block(v, 16), :] = wh
        a = act[2, 1:9, pl.ds(pl.multiple_of(v * 32 + 32, 32), 32), :].reshape(256, 256)
        return pred + lax.dot_general(a, whe[v], NT, preferred_element_type=f32)

    pred = lax.fori_loop(0, 8, predict, jnp.zeros((256, 128), f32), unroll=HU)
    err = ((pred - heat_s[...]) * jnp.concatenate([weight_ref[...]] * 8, axis=0)).astype(bf16)
    err_s[...] = err
    err_t[...] = err.T
    bsum[...] = jnp.zeros_like(bsum)

    def spread(v, gh):
        at = pl.ds(pl.multiple_of(v * 32 + 32, 32), 32)
        a = act[2, 1:9, at, :].reshape(256, 256)
        d = jnp.where(a > 0, dot(err_s[...], whe[v]), 0.0).astype(bf16)
        bsum[2:3, :] += jnp.sum(d.astype(f32), axis=0, keepdims=True)
        grad[2, 1:9, at, :] = d.reshape(8, 32, 256)
        return gh + dot(err_t[block(v, 16), :], a)

    gh = lax.fori_loop(0, 8, spread, jnp.zeros((16, 256), f32), unroll=HV)
    ghead_ref[...] = gh.astype(bf16)
    tail[128:144, :] = 0.5 * head_ref[...] - 0.1 * gh

    m = 8 // UB

    @pl.loop(0, 2 * m)
    def _(k):
        q = k // m
        s = 1 - q
        u = (k - q * m) * UB
        if ONE:
            order = [(i, j) for i in range(3) for j in range(3)]
            rows = [jnp.concatenate([grad[s + 1, u + e + 2 - i, (2 - j) * 32:(2 - j) * 32 + 256, :] for i, j in order], axis=1)
                    for e in range(UB)]
            lhs = rows[0] if UB == 1 else jnp.concatenate(rows, axis=0)
            w = jnp.concatenate(
                [wb[pl.ds(pl.multiple_of(s * 2304 + (3 * i + j) * 256, 256), 256), :] for i, j in order], axis=1)
            da = lax.dot_general(lhs, w, NT, preferred_element_type=f32)
        else:
            da = None
            for i in range(3):
                for j in range(3):
                    ii, jj = 2 - i, 2 - j
                    rows = [grad[s + 1, u + e + ii, jj * 32:jj * 32 + 256, :] for e in range(UB)]
                    lhs = rows[0] if UB == 1 else jnp.concatenate(rows, axis=0)
                    w = wb[pl.ds(pl.multiple_of(s * 2304 + (3 * i + j) * 256, 256), 256), :]
                    t = lax.dot_general(lhs, w, NT, preferred_element_type=f32)
                    da = t if da is None else da + t
        keep = q.astype(f32)
        for e in range(UB):
            d = da[e * 256:(e + 1) * 256] + keep * grad[2, u + e + 1, 32:288, :].astype(f32)
            d = jnp.where(act[s, u + e + 1, 32:288, :] > 0, d, 0.0).astype(bf16)
            grad[s, u + e + 1, 32:288, :] = d
            bsum[pl.ds(s, 1), :] += jnp.sum(d.astype(f32), axis=0, keepdims=True)

    gbias_ref[...] = bsum[0:3, :].astype(bf16)
    tail[144:152, :] = 0.5 * jnp.concatenate([bias_ref[0], bias_ref[1], bias_ref[2], jnp.zeros((5, 256), f32)], axis=0) - 0.1 * bsum[...]
    tail[152:160, :] = jnp.zeros((8, 256), f32)
    gs = dot(x_t[...], grad[0, 1:9, 32:288, :].reshape(2048, 256))
    gstem_ref[...] = gs.astype(bf16)
    tail[0:128, :] = 0.5 * stem_ref[...] - 0.1 * gs
    save_tail = pltpu.make_async_copy(tail, base_hbm.at[pl.ds(ROW_STEM, 160)], tsem)
    save_tail.start()

    load_mine.wait()

    def outs(t):
        r = block(t, 256)
        return (pltpu.make_async_copy(gb.at[r], gconv_hbm.at[r], gsem.at[t]),
                pltpu.make_async_copy(mine.at[r], base_hbm.at[r], osem.at[t]))

    @pl.loop(0, 6)
    def _(q):
        s = q // 3
        j = q - s * 3
        rhs = grad[s + 1, 1:9, 32:288, :].reshape(2048, 256)
        lhs = jnp.concatenate([act_t[s, j, :, i * 256:i * 256 + 2048] for i in range(3)], axis=0)
        all_rows = dot(lhs, rhs)
        for i in range(3):
            t = s * 9 + i * 3 + j
            g = all_rows[i * 256:(i + 1) * 256]
            r = block(t, 256)
            gb[r, :] = g.astype(bf16)
            mine[r, :] = 0.5 * mine[r, :] - 0.1 * g
            for c in outs(t):
                c.start()

    @pl.loop(0, 18)
    def _(t):
        for c in outs(t):
            c.wait()

    save_tail.wait()


def main_call(weight, sel, got, packed, bias, conv, stem, head, U=2, UB=2, HU=8, HV=2, ONE=False):
    vm = pl.BlockSpec(memory_space=pltpu.VMEM)
    hb = pl.BlockSpec(memory_space=pltpu.HBM)
    S = jax.ShapeDtypeStruct
    maps = pltpu.VMEM((3, 10, 320, 256), bf16)
    return pl.pallas_call(
        functools.partial(main_kernel, U=U, UB=UB, HU=HU, HV=HV, ONE=ONE),
        out_shape=(S((4608, 256), bf16), S((PACKED, 256), f32), S((128, 256), bf16), S((16, 256), bf16), S((3, 256), bf16)),
        in_specs=[vm, vm, vm, hb, vm, hb, vm, vm],
        out_specs=(hb, hb, vm, vm, vm),
        scratch_shapes=[
            pltpu.VMEM((PACKED, 256), bf16), pltpu.VMEM((4608, 256), f32), pltpu.VMEM((4608, 256), bf16),
            pltpu.VMEM((128, 2048), bf16), pltpu.VMEM((256, 128), f32), maps, pltpu.VMEM((2, 3, 256, 2560), bf16), maps,
            pltpu.VMEM((8, 128, 256), bf16), pltpu.VMEM((256, 128), bf16), pltpu.VMEM((128, 256), bf16),
            pltpu.VMEM((8, 256), f32), pltpu.VMEM((160, 256), f32),
            pltpu.SemaphoreType.DMA((2,)), pltpu.SemaphoreType.DMA, pltpu.SemaphoreType.DMA, pltpu.SemaphoreType.DMA((18,)), pltpu.SemaphoreType.DMA((18,)),
        ],
        compiler_params=pltpu.CompilerParams(vmem_limit_bytes=48 * 1024 * 1024),
        cost_estimate=pl.CostEstimate(flops=16_000_000_000, bytes_accessed=16_000_000, transcendentals=0),
    )(weight, sel, got, packed, bias, conv, stem, head)


BOTH = ("grp", "dev")
SAME_Z = [[y * 8 + z * 2 + c for y in range(4) for c in range(2)] for z in range(4)]
SAME_Y = [[y * 8 + z * 2 + c for z in range(4) for c in range(2)] for y in range(4)]
Y_BITS = (3, 4)


def prep_kernel(me_ref, step_ref, count_ref, req_hbm, home_hbm, maps_hbm, heat_hbm, asked_ref, sel_ref, weight_ref, mine_ref,
                req, home, heat, maps, wide, sems):
    copies = [
        pltpu.make_async_copy(src, dst, sems.at[k])
        for k, (src, dst) in enumerate((
            (maps_hbm, maps), (heat_hbm, heat), (req_hbm, req), (home_hbm, home),
        ))
    ]
    for c in copies:
        c.start()
    for c in copies[2:]:
        c.wait()
    count = count_ref[0]
    bit = step_ref[0] & 7
    on_y = ((bit == Y_BITS[0]) | (bit == Y_BITS[1])).astype(jnp.int32)
    i = lax.broadcasted_iota(jnp.int32, (32, 32), 0)
    j = lax.broadcasted_iota(jnp.int32, (32, 32), 1)
    wanted = jnp.sum(jnp.where(i == j, req[...], 0), axis=1, keepdims=True)
    lane = lax.broadcasted_iota(jnp.int32, (32, 256), 1)
    pos = jnp.sum(jnp.where(lane == wanted, home[...], 0), axis=1, keepdims=True)
    owner = pos >> 3
    along = 1 + 2 * on_y
    other = 4 - along
    here = (me_ref[0] >> along) & 3
    column = ((owner >> other) & 3) * 2 + (owner & 1)
    row = (((owner >> along) & 3) ^ here) * 8 + (pos & 7)
    across_lanes = jnp.sum(jnp.where(i == j, column, 0), axis=0, keepdims=True)
    live = lax.broadcasted_iota(jnp.int32, (32, 1), 0) < count
    earlier = (across_lanes == column) & (j < i) & (j < count)
    rank = jnp.minimum(jnp.sum(jnp.where(earlier, 1, 0), axis=1, keepdims=True), 7)
    lane64 = lax.broadcasted_iota(jnp.int32, (32, 64), 1)
    pick = jnp.where((lane64 == column * 8 + rank) & live, 1.0, 0.0)
    sel_ref[...] = pick.astype(bf16)
    total = jnp.full((32, 128), count * 1024, jnp.int32).astype(f32)
    weight_ref[...] = jnp.where(lax.broadcasted_iota(jnp.int32, (32, 128), 0) < count, 2.0 / total, 0.0)
    value = jnp.broadcast_to((row + 1).astype(f32), (32, 128)).astype(bf16)
    asked = lax.dot_general(pick.astype(bf16), value, TN, preferred_element_type=f32)
    asked_ref[...] = (asked.astype(jnp.int32) - 1).reshape(8, 8, 128)
    copies[0].wait()
    wide[...] = maps[...].reshape(512, 128).astype(f32)
    for p in range(64):
        mine_ref[:, p * 128:(p + 1) * 128] = wide[pl.ds(p, 8, stride=64), :].astype(bf16)
    copies[1].wait()
    mine_ref[:, 8192:9216] = heat[...]


def prep(me, number, count, req, home, maps, heat):
    vm = pl.BlockSpec(memory_space=pltpu.VMEM)
    sm = pl.BlockSpec(memory_space=pltpu.SMEM)
    hb = pl.BlockSpec(memory_space=pltpu.HBM)
    S = jax.ShapeDtypeStruct
    return pl.pallas_call(
        prep_kernel,
        out_shape=(S((8, 8, 128), jnp.int32), S((32, 64), bf16), S((32, 128), f32), S((8, 9216), bf16)),
        in_specs=[sm, sm, sm, hb, hb, hb, hb],
        out_specs=(vm, vm, vm, vm),
        scratch_shapes=[
            pltpu.VMEM((1, 32), jnp.int32),
            pltpu.VMEM((1, 256), jnp.int32),
            pltpu.VMEM((8, 1024), bf16),
            pltpu.VMEM((8, 64, 128), bf16),
            pltpu.VMEM((512, 128), f32),
            pltpu.SemaphoreType.DMA((4,)),
        ],
        compiler_params=pltpu.CompilerParams(vmem_limit_bytes=60 * 1024 * 1024),
    )(me, number, count, req, home, maps, heat)


def choose_kernel(table_ref, *refs):
    *piles, out_ref = refs
    lane = lax.broadcasted_iota(jnp.int32, (64, 32), 1)
    pick = jnp.where(table_ref[:, 0:32] == lane, 1.0, 0.0).astype(bf16)

    @pl.loop(0, 9)
    def _(k):
        pile = jnp.concatenate([p[:, block(k, 1024)] for p in piles], axis=0)
        out_ref[:, block(k, 1024)] = dot(pick, pile).astype(bf16)


def choose(table, *piles):
    vm = pl.BlockSpec(memory_space=pltpu.VMEM)
    return pl.pallas_call(
        choose_kernel,
        out_shape=jax.ShapeDtypeStruct((64, 9216), bf16),
        in_specs=[vm] * 5,
        out_specs=vm,
        compiler_params=pltpu.CompilerParams(vmem_limit_bytes=8 * 1024 * 1024),
        cost_estimate=pl.CostEstimate(flops=40000000, bytes_accessed=2000000, transcendentals=0),
    )(table, *piles)


PARTS = 6
PART = 4608 // PARTS


def pack_kernel(conv_hbm, stem_hbm, head_hbm, bias_hbm, out_hbm, wide, bias, narrow, isem, osem):
    def load(k):
        r = block(k, PART)
        return pltpu.make_async_copy(conv_hbm.at[r], wide.at[r], isem.at[k])

    def save(k):
        r = block(k, PART)
        return pltpu.make_async_copy(narrow.at[r], out_hbm.at[r], osem.at[k])

    def save_tail():
        r = pl.ds(ROW_STEM, 160)
        return pltpu.make_async_copy(narrow.at[r], out_hbm.at[r], osem.at[PARTS])

    small = [
        pltpu.make_async_copy(stem_hbm, wide.at[pl.ds(ROW_STEM, 128)], isem.at[PARTS]),
        pltpu.make_async_copy(head_hbm, wide.at[pl.ds(ROW_HEAD, 16)], isem.at[PARTS + 1]),
        pltpu.make_async_copy(bias_hbm, bias, isem.at[PARTS + 2]),
    ]
    for k in range(PARTS):
        load(k).start()
    for c in small:
        c.start()

    def narrowed(lo, n):
        @pl.loop(0, n // 48)
        def _(q):
            r = pl.ds(pl.multiple_of(lo + q * 48, 16), 48)
            narrow[r, :] = wide[r, :].astype(bf16)

    @pl.loop(0, PARTS)
    def _(k):
        load(k).wait()
        narrowed(k * PART, PART)
        save(k).start()

    for c in small:
        c.wait()
    narrowed(ROW_STEM, 144)
    narrow[ROW_STEM + 144:PACKED, :] = jnp.concatenate([bias[0], bias[1], bias[2], jnp.zeros((13, 256), f32)], axis=0).astype(bf16)
    save_tail().start()

    @pl.loop(0, PARTS)
    def _(k):
        save(k).wait()

    save_tail().wait()


def pack(conv, stem, head, bias):
    hb = pl.BlockSpec(memory_space=pltpu.HBM)
    return pl.pallas_call(
        pack_kernel,
        out_shape=jax.ShapeDtypeStruct((PACKED, 256), bf16),
        in_specs=[hb, hb, hb, hb],
        out_specs=hb,
        scratch_shapes=[
            pltpu.VMEM((PACKED, 256), f32),
            pltpu.VMEM((3, 1, 256), f32),
            pltpu.VMEM((PACKED, 256), bf16),
            pltpu.SemaphoreType.DMA((PARTS + 3,)),
            pltpu.SemaphoreType.DMA((PARTS + 1,)),
        ],
        compiler_params=pltpu.CompilerParams(vmem_limit_bytes=16 * 1024 * 1024),
        cost_estimate=pl.CostEstimate(flops=1000000, bytes_accessed=7000000, transcendentals=0),
    )(conv, stem, head, bias)


MIX = 8
PIECE = 4608 // MIX


def mix_kernel(t_hbm, base_hbm, new_hbm, nstem_hbm, nhead_hbm, nbias_ref, theirs, wide, asem, bsem, osem):
    def loads(k, r):
        return (pltpu.make_async_copy(t_hbm.at[r], theirs.at[r], asem.at[k]),
                pltpu.make_async_copy(base_hbm.at[r], wide.at[r], bsem.at[k]))

    def save(k):
        r = block(k, PIECE)
        return pltpu.make_async_copy(wide.at[r], new_hbm.at[r], osem.at[k])

    last = loads(MIX, pl.ds(ROW_STEM, 160))
    for c in last:
        c.start()
    for k in range(MIX):
        for c in loads(k, block(k, PIECE)):
            c.start()

    def mixed(lo, n):
        @pl.loop(0, n // 32)
        def _(q):
            r = pl.ds(pl.multiple_of(lo + q * 32, 32), 32)
            wide[r, :] = wide[r, :] + 0.5 * theirs[r, :].astype(f32)

    for c in last:
        c.wait()
    mixed(ROW_STEM, 160)
    small = (pltpu.make_async_copy(wide.at[pl.ds(ROW_STEM, 128)], nstem_hbm, osem.at[MIX]),
             pltpu.make_async_copy(wide.at[pl.ds(ROW_HEAD, 16)], nhead_hbm, osem.at[MIX + 1]))
    for c in small:
        c.start()
    for k in range(3):
        nbias_ref[k] = wide[ROW_HEAD + 16 + k:ROW_HEAD + 17 + k, :]

    @pl.loop(0, MIX)
    def _(k):
        for c in loads(k, block(k, PIECE)):
            c.wait()
        mixed(k * PIECE, PIECE)
        save(k).start()

    @pl.loop(0, MIX)
    def _(k):
        save(k).wait()

    for c in small:
        c.wait()


def mix(theirs, base):
    vm = pl.BlockSpec(memory_space=pltpu.VMEM)
    hb = pl.BlockSpec(memory_space=pltpu.HBM)
    S = jax.ShapeDtypeStruct
    return pl.pallas_call(
        mix_kernel,
        out_shape=(S((4608, 256), f32), S((128, 256), f32), S((16, 256), f32), S((3, 1, 256), f32)),
        in_specs=[hb, hb],
        out_specs=(hb, hb, hb, vm),
        scratch_shapes=[
            pltpu.VMEM((PACKED, 256), bf16),
            pltpu.VMEM((PACKED, 256), f32),
            pltpu.SemaphoreType.DMA((MIX + 1,)),
            pltpu.SemaphoreType.DMA((MIX + 1,)),
            pltpu.SemaphoreType.DMA((MIX + 2,)),
        ],
        compiler_params=pltpu.CompilerParams(vmem_limit_bytes=16 * 1024 * 1024),
        cost_estimate=pl.CostEstimate(flops=1000000, bytes_accessed=12000000, transcendentals=0),
    )(theirs, base)


def swap(array, bit):
    return lax.ppermute(array, BOTH, [(i, i ^ (1 << bit)) for i in range(256)])


def among(array, groups):
    return lax.all_to_all(array, "dev", split_axis=0, concat_axis=0, axis_index_groups=groups, tiled=True)


def gather(on_y, asked, mine, conv, stem, head, bias):
    shift, groups = (3, SAME_Y) if on_y else (1, SAME_Z)
    others = [lax.ppermute(mine, "dev", [(i, i ^ (m << shift)) for i in range(32)]) for m in (1, 2, 3)]
    table = among(asked, groups)
    packed = pack(conv, stem, head, bias)
    send = choose(table.reshape(64, 128), mine, *others)
    return packed, send


def step(bit, weight, sel, send, packed, bias, conv, stem, head):
    theirs = swap(packed, bit)
    got = among(send, SAME_Y if bit in Y_BITS else SAME_Z)
    outs = main_call(weight, sel, got.reshape(64, 9216), packed, bias, conv, stem, head)
    return (theirs, *outs)


def local(step_number, maps, heat, home, requests, counts, stem, conv, head, bias):
    stem, conv, head, bias = stem[0], conv.reshape(4608, 256), head[0], jnp.transpose(bias, (1, 0, 2))
    bit = step_number & 7
    on_y = ((bit == Y_BITS[0]) | (bit == Y_BITS[1])).astype(jnp.int32)
    me = lax.axis_index("dev").astype(jnp.int32)
    asked, sel, weight, mine = prep(me.reshape(1), step_number.reshape(1), counts, requests, home, maps, heat)
    packed, send = lax.switch(
        on_y, [functools.partial(gather, 0), functools.partial(gather, 1)],
        asked, mine, conv, stem, head, bias,
    )
    outs = lax.switch(
        bit, [functools.partial(step, b) for b in range(8)],
        weight, sel, send.reshape(8, 8, 9216), packed, bias, conv, stem, head,
    )
    theirs, gconv, base, gstem, ghead, gbias = outs
    new, nstem, nhead, nbias = mix(theirs, base)
    return (
        nstem[None], new.reshape(1, 2, 2304, 256), nhead[None], jnp.transpose(nbias, (1, 0, 2)),
        gstem[None], gconv.reshape(1, 2, 2304, 256), ghead[None], gbias[None],
    )


def solution(mesh):
    placed = (
        P(),
        P(BOTH, None, None),
        P(BOTH, None),
        P("grp", None),
        P(BOTH, None),
        P(BOTH),
        P(BOTH, None, None),
        P(BOTH, None, None, None),
        P(BOTH, None, None),
        P(BOTH, None, None),
    )
    outs = (
        P(BOTH, None, None),
        P(BOTH, None, None, None),
        P(BOTH, None, None),
        P(BOTH, None, None),
        P(BOTH, None, None),
        P(BOTH, None, None, None),
        P(BOTH, None, None),
        P(BOTH, None, None),
    )
    return jax.shard_map(local, mesh=mesh, in_specs=placed, out_specs=outs, check_vma=False)
```

```python
import functools

import jax
import jax.numpy as jnp
from jax import lax
from jax.experimental import pallas as pl
from jax.experimental.pallas import tpu as pltpu
from jax.sharding import PartitionSpec as P


bf16 = jnp.bfloat16
f32 = jnp.float32
NT = (((1,), (1,)), ((), ()))
TN = (((0,), (0,)), ((), ()))
ROW_STEM = 4608
ROW_HEAD = 4736
PACKED = 4768


def dot(a, b):
    return jnp.dot(a, b, preferred_element_type=f32)


def block(i, n):
    return pl.ds(pl.multiple_of(i * n, n), n)


def main_kernel(
    weight_ref, sel_ref, got_ref, w_hbm, bias_ref, conv_hbm, stem_ref, head_ref,
    gconv_hbm, base_ref, gstem_ref, ghead_ref, gbias_ref,
    wb, mine, gb, x_t, heat_s, act, act_t, grad, whe, err_s, err_t, bsum,
    wsem, msem, gsem, *, U, UB, HU, HV, ONE):
    wcopies = []
    for k, (lo, n) in enumerate(((ROW_STEM, PACKED - ROW_STEM), (0, ROW_STEM))):
        c = pltpu.make_async_copy(w_hbm.at[pl.ds(lo, n)], wb.at[pl.ds(lo, n)], wsem.at[k])
        c.start()
        wcopies.append(c)
    load_mine = pltpu.make_async_copy(conv_hbm, mine, msem)

    edge = jnp.zeros((32, 256), bf16)

    @pl.loop(0, 10)
    def _(q):
        for buf, ks in ((act, (0, 1)), (grad, (1, 2))):
            for k in ks:
                buf[k, 0, block(q, 32), :] = edge
                buf[k, 9, block(q, 32), :] = edge
                buf[k, q, 0:32, :] = edge
                buf[k, q, 288:320, :] = edge

    @pl.loop(0, 6)
    def _(q):
        z = jnp.zeros((256, 256), bf16)
        act_t[q // 3, q % 3, :, 0:256] = z
        act_t[q // 3, q % 3, :, 2304:2560] = z

    sel = sel_ref[...]
    wcopies[0].wait()
    ws = wb[ROW_STEM:ROW_STEM + 128, :]
    b0 = bias_ref[0]

    @pl.loop(0, 8)
    def _(u):
        r = dot(sel, got_ref[:, block(u, 1024)]).astype(bf16)
        x = jnp.concatenate([r[:, v * 128:(v + 1) * 128] for v in range(8)], axis=0)
        x_t[:, block(u, 256)] = x.T
        heat_s[block(u, 32), :] = dot(sel, got_ref[:, pl.ds(pl.multiple_of(8192 + u * 128, 128), 128)])
        pre = dot(x, ws) + b0
        a = jnp.maximum(pre, 0.0).astype(bf16)
        act[0, u + 1, 32:288, :] = a

    wcopies[1].wait()
    load_mine.start()
    n = 8 // U

    @pl.loop(0, 2 * n)
    def _(k):
        s = k // n
        u = (k - s * n) * U
        rows = []
        for e in range(U):
            rows.append(jnp.concatenate(
                [act[s, u + e + i, j * 32:j * 32 + 256, :] for i in range(3) for j in range(3)], axis=1))
        lhs = rows[0] if U == 1 else jnp.concatenate(rows, axis=0)
        pre = dot(lhs, wb[block(s, 2304), :]) + bias_ref[s + 1]
        for e in range(U):
            for j in range(3):
                act_t[s, j, :, block(u + e + 1, 256)] = act[s, u + e + 1, j * 32:j * 32 + 256, :].T
        keep = s.astype(f32)
        for e in range(U):
            p = pre[e * 256:(e + 1) * 256] + keep * act[0, u + e + 1, 32:288, :].astype(f32)
            a = jnp.maximum(p, 0.0).astype(bf16)
            act[s + 1, u + e + 1, 32:288, :] = a

    wh = wb[ROW_HEAD:ROW_HEAD + 16, :]

    def predict(v, pred):
        whe[v] = jnp.zeros((128, 256), bf16)
        whe[v, block(v, 16), :] = wh
        a = act[2, 1:9, pl.ds(pl.multiple_of(v * 32 + 32, 32), 32), :].reshape(256, 256)
        return pred + lax.dot_general(a, whe[v], NT, preferred_element_type=f32)

    pred = lax.fori_loop(0, 8, predict, jnp.zeros((256, 128), f32), unroll=HU)
    err = ((pred - heat_s[...]) * jnp.concatenate([weight_ref[...]] * 8, axis=0)).astype(bf16)
    err_s[...] = err
    err_t[...] = err.T
    bsum[...] = jnp.zeros_like(bsum)

    def spread(v, gh):
        at = pl.ds(pl.multiple_of(v * 32 + 32, 32), 32)
        a = act[2, 1:9, at, :].reshape(256, 256)
        d = jnp.where(a > 0, dot(err_s[...], whe[v]), 0.0).astype(bf16)
        bsum[2:3, :] += jnp.sum(d.astype(f32), axis=0, keepdims=True)
        grad[2, 1:9, at, :] = d.reshape(8, 32, 256)
        return gh + dot(err_t[block(v, 16), :], a)

    gh = lax.fori_loop(0, 8, spread, jnp.zeros((16, 256), f32), unroll=HV)
    ghead_ref[...] = gh.astype(bf16)
    base_ref[ROW_HEAD:ROW_HEAD + 16, :] = 0.5 * head_ref[...] - 0.1 * gh

    m = 8 // UB

    @pl.loop(0, 2 * m)
    def _(k):
        q = k // m
        s = 1 - q
        u = (k - q * m) * UB
        if ONE:
            order = [(i, j) for i in range(3) for j in range(3)]
            rows = [jnp.concatenate([grad[s + 1, u + e + 2 - i, (2 - j) * 32:(2 - j) * 32 + 256, :] for i, j in order], axis=1)
                    for e in range(UB)]
            lhs = rows[0] if UB == 1 else jnp.concatenate(rows, axis=0)
            w = jnp.concatenate(
                [wb[pl.ds(pl.multiple_of(s * 2304 + (3 * i + j) * 256, 256), 256), :] for i, j in order], axis=1)
            da = lax.dot_general(lhs, w, NT, preferred_element_type=f32)
        else:
            da = None
            for i in range(3):
                for j in range(3):
                    ii, jj = 2 - i, 2 - j
                    rows = [grad[s + 1, u + e + ii, jj * 32:jj * 32 + 256, :] for e in range(UB)]
                    lhs = rows[0] if UB == 1 else jnp.concatenate(rows, axis=0)
                    w = wb[pl.ds(pl.multiple_of(s * 2304 + (3 * i + j) * 256, 256), 256), :]
                    t = lax.dot_general(lhs, w, NT, preferred_element_type=f32)
                    da = t if da is None else da + t
        keep = q.astype(f32)
        for e in range(UB):
            d = da[e * 256:(e + 1) * 256] + keep * grad[2, u + e + 1, 32:288, :].astype(f32)
            d = jnp.where(act[s, u + e + 1, 32:288, :] > 0, d, 0.0).astype(bf16)
            grad[s, u + e + 1, 32:288, :] = d
            bsum[pl.ds(s, 1), :] += jnp.sum(d.astype(f32), axis=0, keepdims=True)

    gbias_ref[...] = bsum[0:3, :].astype(bf16)
    base_ref[ROW_HEAD + 16:ROW_HEAD + 24, :] = 0.5 * jnp.concatenate([bias_ref[0], bias_ref[1], bias_ref[2], jnp.zeros((5, 256), f32)], axis=0) - 0.1 * bsum[...]
    base_ref[ROW_HEAD + 24:PACKED, :] = jnp.zeros((8, 256), f32)
    gs = dot(x_t[...], grad[0, 1:9, 32:288, :].reshape(2048, 256))
    gstem_ref[...] = gs.astype(bf16)
    base_ref[ROW_STEM:ROW_HEAD, :] = 0.5 * stem_ref[...] - 0.1 * gs

    load_mine.wait()

    def outs(t):
        r = block(t, 256)
        return (pltpu.make_async_copy(gb.at[r], gconv_hbm.at[r], gsem.at[t]),)

    @pl.loop(0, 6)
    def _(q):
        s = q // 3
        j = q - s * 3
        rhs = grad[s + 1, 1:9, 32:288, :].reshape(2048, 256)
        lhs = jnp.concatenate([act_t[s, j, :, i * 256:i * 256 + 2048] for i in range(3)], axis=0)
        all_rows = dot(lhs, rhs)
        for i in range(3):
            t = s * 9 + i * 3 + j
            g = all_rows[i * 256:(i + 1) * 256]
            r = block(t, 256)
            gb[r, :] = g.astype(bf16)
            base_ref[r, :] = 0.5 * mine[r, :] - 0.1 * g
            for c in outs(t):
                c.start()

    @pl.loop(0, 18)
    def _(t):
        for c in outs(t):
            c.wait()


def main_call(weight, sel, got, packed, bias, conv, stem, head, U=2, UB=2, HU=8, HV=4, ONE=False):
    vm = pl.BlockSpec(memory_space=pltpu.VMEM)
    hb = pl.BlockSpec(memory_space=pltpu.HBM)
    S = jax.ShapeDtypeStruct
    maps = pltpu.VMEM((3, 10, 320, 256), bf16)
    return pl.pallas_call(
        functools.partial(main_kernel, U=U, UB=UB, HU=HU, HV=HV, ONE=ONE),
        out_shape=(S((4608, 256), bf16), S((PACKED, 256), f32), S((128, 256), bf16), S((16, 256), bf16), S((3, 256), bf16)),
        in_specs=[vm, vm, vm, hb, vm, hb, vm, vm],
        out_specs=(hb, vm, vm, vm, vm),
        scratch_shapes=[
            pltpu.VMEM((PACKED, 256), bf16), pltpu.VMEM((4608, 256), f32), pltpu.VMEM((4608, 256), bf16),
            pltpu.VMEM((128, 2048), bf16), pltpu.VMEM((256, 128), f32), maps, pltpu.VMEM((2, 3, 256, 2560), bf16), maps,
            pltpu.VMEM((8, 128, 256), bf16), pltpu.VMEM((256, 128), bf16), pltpu.VMEM((128, 256), bf16),
            pltpu.VMEM((8, 256), f32),
            pltpu.SemaphoreType.DMA((2,)), pltpu.SemaphoreType.DMA, pltpu.SemaphoreType.DMA((18,)),
        ],
        compiler_params=pltpu.CompilerParams(vmem_limit_bytes=48 * 1024 * 1024),
        cost_estimate=pl.CostEstimate(flops=16_000_000_000, bytes_accessed=16_000_000, transcendentals=0),
    )(weight, sel, got, packed, bias, conv, stem, head)


BOTH = ("grp", "dev")
SAME_Z = [[y * 8 + z * 2 + c for y in range(4) for c in range(2)] for z in range(4)]
SAME_Y = [[y * 8 + z * 2 + c for z in range(4) for c in range(2)] for y in range(4)]
Y_BITS = (3, 4)


def prep_kernel(me_ref, step_ref, count_ref, req_hbm, home_hbm, maps_hbm, heat_hbm, asked_ref, sel_ref, weight_ref, mine_ref,
                req, home, heat, maps, wide, sems):
    copies = [
        pltpu.make_async_copy(src, dst, sems.at[k])
        for k, (src, dst) in enumerate((
            (maps_hbm, maps), (heat_hbm, heat), (req_hbm, req), (home_hbm, home),
        ))
    ]
    for c in copies:
        c.start()
    for c in copies[2:]:
        c.wait()
    count = count_ref[0]
    bit = step_ref[0] & 7
    on_y = ((bit == Y_BITS[0]) | (bit == Y_BITS[1])).astype(jnp.int32)
    i = lax.broadcasted_iota(jnp.int32, (32, 32), 0)
    j = lax.broadcasted_iota(jnp.int32, (32, 32), 1)
    wanted = jnp.sum(jnp.where(i == j, req[...], 0), axis=1, keepdims=True)
    lane = lax.broadcasted_iota(jnp.int32, (32, 256), 1)
    pos = jnp.sum(jnp.where(lane == wanted, home[...], 0), axis=1, keepdims=True)
    owner = pos >> 3
    along = 1 + 2 * on_y
    other = 4 - along
    here = (me_ref[0] >> along) & 3
    column = ((owner >> other) & 3) * 2 + (owner & 1)
    row = (((owner >> along) & 3) ^ here) * 8 + (pos & 7)
    across_lanes = jnp.sum(jnp.where(i == j, column, 0), axis=0, keepdims=True)
    live = lax.broadcasted_iota(jnp.int32, (32, 1), 0) < count
    earlier = (across_lanes == column) & (j < i) & (j < count)
    rank = jnp.minimum(jnp.sum(jnp.where(earlier, 1, 0), axis=1, keepdims=True), 7)
    lane64 = lax.broadcasted_iota(jnp.int32, (32, 64), 1)
    pick = jnp.where((lane64 == column * 8 + rank) & live, 1.0, 0.0)
    sel_ref[...] = pick.astype(bf16)
    total = jnp.full((32, 128), count * 1024, jnp.int32).astype(f32)
    weight_ref[...] = jnp.where(lax.broadcasted_iota(jnp.int32, (32, 128), 0) < count, 2.0 / total, 0.0)
    value = jnp.broadcast_to((row + 1).astype(f32), (32, 128)).astype(bf16)
    asked = lax.dot_general(pick.astype(bf16), value, TN, preferred_element_type=f32)
    asked_ref[...] = (asked.astype(jnp.int32) - 1).reshape(8, 8, 128)
    copies[0].wait()
    wide[...] = maps[...].reshape(512, 128).astype(f32)
    for p in range(64):
        mine_ref[:, p * 128:(p + 1) * 128] = wide[pl.ds(p, 8, stride=64), :].astype(bf16)
    copies[1].wait()
    mine_ref[:, 8192:9216] = heat[...]


def prep(me, number, count, req, home, maps, heat):
    vm = pl.BlockSpec(memory_space=pltpu.VMEM)
    sm = pl.BlockSpec(memory_space=pltpu.SMEM)
    hb = pl.BlockSpec(memory_space=pltpu.HBM)
    S = jax.ShapeDtypeStruct
    return pl.pallas_call(
        prep_kernel,
        out_shape=(S((8, 8, 128), jnp.int32), S((32, 64), bf16), S((32, 128), f32), S((8, 9216), bf16)),
        in_specs=[sm, sm, sm, hb, hb, hb, hb],
        out_specs=(vm, vm, vm, vm),
        scratch_shapes=[
            pltpu.VMEM((1, 32), jnp.int32),
            pltpu.VMEM((1, 256), jnp.int32),
            pltpu.VMEM((8, 1024), bf16),
            pltpu.VMEM((8, 64, 128), bf16),
            pltpu.VMEM((512, 128), f32),
            pltpu.SemaphoreType.DMA((4,)),
        ],
        compiler_params=pltpu.CompilerParams(vmem_limit_bytes=60 * 1024 * 1024),
    )(me, number, count, req, home, maps, heat)


def choose_kernel(table_ref, *refs):
    *piles, out_ref = refs
    lane = lax.broadcasted_iota(jnp.int32, (64, 32), 1)
    pick = jnp.where(table_ref[:, 0:32] == lane, 1.0, 0.0).astype(bf16)

    @pl.loop(0, 9)
    def _(k):
        pile = jnp.concatenate([p[:, block(k, 1024)] for p in piles], axis=0)
        out_ref[:, block(k, 1024)] = dot(pick, pile).astype(bf16)


def choose(table, *piles):
    vm = pl.BlockSpec(memory_space=pltpu.VMEM)
    return pl.pallas_call(
        choose_kernel,
        out_shape=jax.ShapeDtypeStruct((64, 9216), bf16),
        in_specs=[vm] * 5,
        out_specs=vm,
        compiler_params=pltpu.CompilerParams(vmem_limit_bytes=8 * 1024 * 1024),
        cost_estimate=pl.CostEstimate(flops=40000000, bytes_accessed=2000000, transcendentals=0),
    )(table, *piles)


PARTS = 6
PART = 4608 // PARTS


def pack_kernel(conv_hbm, stem_hbm, head_hbm, bias_hbm, out_hbm, wide, bias, narrow, isem, osem):
    def load(k):
        r = block(k, PART)
        return pltpu.make_async_copy(conv_hbm.at[r], wide.at[r], isem.at[k])

    def save(k):
        r = block(k, PART)
        return pltpu.make_async_copy(narrow.at[r], out_hbm.at[r], osem.at[k])

    def save_tail():
        r = pl.ds(ROW_STEM, 160)
        return pltpu.make_async_copy(narrow.at[r], out_hbm.at[r], osem.at[PARTS])

    small = [
        pltpu.make_async_copy(stem_hbm, wide.at[pl.ds(ROW_STEM, 128)], isem.at[PARTS]),
        pltpu.make_async_copy(head_hbm, wide.at[pl.ds(ROW_HEAD, 16)], isem.at[PARTS + 1]),
        pltpu.make_async_copy(bias_hbm, bias, isem.at[PARTS + 2]),
    ]
    for k in range(PARTS):
        load(k).start()
    for c in small:
        c.start()

    def narrowed(lo, n):
        @pl.loop(0, n // 48)
        def _(q):
            r = pl.ds(pl.multiple_of(lo + q * 48, 16), 48)
            narrow[r, :] = wide[r, :].astype(bf16)

    @pl.loop(0, PARTS)
    def _(k):
        load(k).wait()
        narrowed(k * PART, PART)
        save(k).start()

    for c in small:
        c.wait()
    narrowed(ROW_STEM, 144)
    narrow[ROW_STEM + 144:PACKED, :] = jnp.concatenate([bias[0], bias[1], bias[2], jnp.zeros((13, 256), f32)], axis=0).astype(bf16)
    save_tail().start()

    @pl.loop(0, PARTS)
    def _(k):
        save(k).wait()

    save_tail().wait()


def pack(conv, stem, head, bias):
    hb = pl.BlockSpec(memory_space=pltpu.HBM)
    return pl.pallas_call(
        pack_kernel,
        out_shape=jax.ShapeDtypeStruct((PACKED, 256), bf16),
        in_specs=[hb, hb, hb, hb],
        out_specs=hb,
        scratch_shapes=[
            pltpu.VMEM((PACKED, 256), f32),
            pltpu.VMEM((3, 1, 256), f32),
            pltpu.VMEM((PACKED, 256), bf16),
            pltpu.SemaphoreType.DMA((PARTS + 3,)),
            pltpu.SemaphoreType.DMA((PARTS + 1,)),
        ],
        compiler_params=pltpu.CompilerParams(vmem_limit_bytes=16 * 1024 * 1024),
        cost_estimate=pl.CostEstimate(flops=1000000, bytes_accessed=7000000, transcendentals=0),
    )(conv, stem, head, bias)


PIECES = ((0, 256), (256, 512), (768, 768), (1536, 1024), (2560, 1024), (3584, 640), (4224, 384))


def mix_kernel(t_hbm, base_ref, new_hbm, nstem_hbm, nhead_hbm, nbias_ref, theirs, wide, asem, osem):
    def load(k, lo, n):
        return pltpu.make_async_copy(t_hbm.at[pl.ds(lo, n)], theirs.at[pl.ds(lo, n)], asem.at[k])

    def mixed(lo, n):
        @pl.loop(0, n // 32)
        def _(q):
            r = pl.ds(pl.multiple_of(lo + q * 32, 32), 32)
            wide[r, :] = base_ref[r, :] + 0.5 * theirs[r, :].astype(f32)

    loads = [load(k, lo, n) for k, (lo, n) in enumerate(PIECES + ((ROW_STEM, 160),))]
    for c in loads:
        c.start()
    saves = []
    for k, (lo, n) in enumerate(PIECES):
        loads[k].wait()
        mixed(lo, n)
        saves.append(pltpu.make_async_copy(wide.at[pl.ds(lo, n)], new_hbm.at[pl.ds(lo, n)], osem.at[k]))
        saves[-1].start()
    loads[-1].wait()
    mixed(ROW_STEM, 160)
    last = len(PIECES)
    saves.append(pltpu.make_async_copy(wide.at[pl.ds(ROW_STEM, 128)], nstem_hbm, osem.at[last]))
    saves.append(pltpu.make_async_copy(wide.at[pl.ds(ROW_HEAD, 16)], nhead_hbm, osem.at[last + 1]))
    for c in saves[-2:]:
        c.start()
    for k in range(3):
        nbias_ref[k] = wide[ROW_HEAD + 16 + k:ROW_HEAD + 17 + k, :]
    for c in saves:
        c.wait()


def mix(theirs, base):
    vm = pl.BlockSpec(memory_space=pltpu.VMEM)
    hb = pl.BlockSpec(memory_space=pltpu.HBM)
    S = jax.ShapeDtypeStruct
    return pl.pallas_call(
        mix_kernel,
        out_shape=(S((4608, 256), f32), S((128, 256), f32), S((16, 256), f32), S((3, 1, 256), f32)),
        in_specs=[hb, vm],
        out_specs=(hb, hb, hb, vm),
        scratch_shapes=[
            pltpu.VMEM((PACKED, 256), bf16),
            pltpu.VMEM((PACKED, 256), f32),
            pltpu.SemaphoreType.DMA((len(PIECES) + 1,)),
            pltpu.SemaphoreType.DMA((len(PIECES) + 2,)),
        ],
        compiler_params=pltpu.CompilerParams(vmem_limit_bytes=24 * 1024 * 1024),
        cost_estimate=pl.CostEstimate(flops=1000000, bytes_accessed=12000000, transcendentals=0),
    )(theirs, base)


def swap(array, bit):
    return lax.ppermute(array, BOTH, [(i, i ^ (1 << bit)) for i in range(256)])


def among(array, groups):
    return lax.all_to_all(array, "dev", split_axis=0, concat_axis=0, axis_index_groups=groups, tiled=True)


def gather(on_y, asked, mine, conv, stem, head, bias):
    shift, groups = (3, SAME_Y) if on_y else (1, SAME_Z)
    others = [lax.ppermute(mine, "dev", [(i, i ^ (m << shift)) for i in range(32)]) for m in (1, 2, 3)]
    table = among(asked, groups)
    packed = pack(conv, stem, head, bias)
    return packed, table, *others


def step(bit, weight, sel, table, mine, one, two, three, packed, bias, conv, stem, head):
    theirs = swap(packed, bit)
    send = choose(table.reshape(64, 128), mine, one, two, three).reshape(8, 8, 9216)
    got = among(send, SAME_Y if bit in Y_BITS else SAME_Z)
    outs = main_call(weight, sel, got.reshape(64, 9216), packed, bias, conv, stem, head)
    return (theirs, *outs)


def local(step_number, maps, heat, home, requests, counts, stem, conv, head, bias):
    stem, conv, head, bias = stem[0], conv.reshape(4608, 256), head[0], jnp.transpose(bias, (1, 0, 2))
    bit = step_number & 7
    on_y = ((bit == Y_BITS[0]) | (bit == Y_BITS[1])).astype(jnp.int32)
    me = lax.axis_index("dev").astype(jnp.int32)
    asked, sel, weight, mine = prep(me.reshape(1), step_number.reshape(1), counts, requests, home, maps, heat)
    packed, table, *others = lax.switch(
        on_y, [functools.partial(gather, 0), functools.partial(gather, 1)],
        asked, mine, conv, stem, head, bias,
    )
    outs = lax.switch(
        bit, [functools.partial(step, b) for b in range(8)],
        weight, sel, table, mine, *others, packed, bias, conv, stem, head,
    )
    theirs, gconv, base, gstem, ghead, gbias = outs
    new, nstem, nhead, nbias = mix(theirs, base)
    return (
        nstem[None], new.reshape(1, 2, 2304, 256), nhead[None], jnp.transpose(nbias, (1, 0, 2)),
        gstem[None], gconv.reshape(1, 2, 2304, 256), ghead[None], gbias[None],
    )


def solution(mesh):
    placed = (
        P(),
        P(BOTH, None, None),
        P(BOTH, None),
        P("grp", None),
        P(BOTH, None),
        P(BOTH),
        P(BOTH, None, None),
        P(BOTH, None, None, None),
        P(BOTH, None, None),
        P(BOTH, None, None),
    )
    outs = (
        P(BOTH, None, None),
        P(BOTH, None, None, None),
        P(BOTH, None, None),
        P(BOTH, None, None),
        P(BOTH, None, None),
        P(BOTH, None, None, None),
        P(BOTH, None, None),
        P(BOTH, None, None),
    )
    return jax.shard_map(local, mesh=mesh, in_specs=placed, out_specs=outs, check_vma=False)
```

```python
import functools

import jax
import jax.numpy as jnp
from jax import lax
from jax.experimental import pallas as pl
from jax.experimental.pallas import tpu as pltpu
from jax.sharding import PartitionSpec as P


bf16 = jnp.bfloat16
f32 = jnp.float32
NT = (((1,), (1,)), ((), ()))
TN = (((0,), (0,)), ((), ()))
ROW_STEM = 4608
ROW_HEAD = 4736
PACKED = 4768


def dot(a, b):
    return jnp.dot(a, b, preferred_element_type=f32)


def block(i, n):
    return pl.ds(pl.multiple_of(i * n, n), n)


def main_kernel(
    weight_ref, sel_ref, got_ref, w_hbm, bias_ref, conv_hbm, stem_ref, head_ref,
    gconv_hbm, base_ref, gstem_ref, ghead_ref, gbias_ref,
    wb, mine, gb, x_t, heat_s, act, act_t, grad, whe, err_s, err_t, bsum,
    wsem, msem, gsem, *, U, UB, HU, HV, ONE):
    wcopies = []
    for k, (lo, n) in enumerate(((ROW_STEM, PACKED - ROW_STEM), (0, ROW_STEM))):
        c = pltpu.make_async_copy(w_hbm.at[pl.ds(lo, n)], wb.at[pl.ds(lo, n)], wsem.at[k])
        c.start()
        wcopies.append(c)
    load_mine = pltpu.make_async_copy(conv_hbm, mine, msem)

    edge = jnp.zeros((32, 256), bf16)

    @pl.loop(0, 10)
    def _(q):
        for buf, ks in ((act, (0, 1)), (grad, (1, 2))):
            for k in ks:
                buf[k, 0, block(q, 32), :] = edge
                buf[k, 9, block(q, 32), :] = edge
                buf[k, q, 0:32, :] = edge
                buf[k, q, 288:320, :] = edge

    @pl.loop(0, 6)
    def _(q):
        z = jnp.zeros((256, 256), bf16)
        act_t[q // 3, q % 3, :, 0:256] = z
        act_t[q // 3, q % 3, :, 2304:2560] = z

    sel = sel_ref[...]
    wcopies[0].wait()
    ws = wb[ROW_STEM:ROW_STEM + 128, :]
    b0 = bias_ref[0]

    @pl.loop(0, 8)
    def _(u):
        r = dot(sel, got_ref[:, block(u, 1024)]).astype(bf16)
        x = jnp.concatenate([r[:, v * 128:(v + 1) * 128] for v in range(8)], axis=0)
        x_t[:, block(u, 256)] = x.T
        heat_s[block(u, 32), :] = dot(sel, got_ref[:, pl.ds(pl.multiple_of(8192 + u * 128, 128), 128)])
        pre = dot(x, ws) + b0
        a = jnp.maximum(pre, 0.0).astype(bf16)
        act[0, u + 1, 32:288, :] = a

    wcopies[1].wait()
    load_mine.start()
    n = 8 // U

    @pl.loop(0, 2 * n)
    def _(k):
        s = k // n
        u = (k - s * n) * U
        rows = []
        for e in range(U):
            rows.append(jnp.concatenate(
                [act[s, u + e + i, j * 32:j * 32 + 256, :] for i in range(3) for j in range(3)], axis=1))
        lhs = rows[0] if U == 1 else jnp.concatenate(rows, axis=0)
        pre = dot(lhs, wb[block(s, 2304), :]) + bias_ref[s + 1]
        for e in range(U):
            for j in range(3):
                act_t[s, j, :, block(u + e + 1, 256)] = act[s, u + e + 1, j * 32:j * 32 + 256, :].T
        keep = s.astype(f32)
        for e in range(U):
            p = pre[e * 256:(e + 1) * 256] + keep * act[0, u + e + 1, 32:288, :].astype(f32)
            a = jnp.maximum(p, 0.0).astype(bf16)
            act[s + 1, u + e + 1, 32:288, :] = a

    wh = wb[ROW_HEAD:ROW_HEAD + 16, :]

    def predict(v, pred):
        whe[v] = jnp.zeros((128, 256), bf16)
        whe[v, block(v, 16), :] = wh
        a = act[2, 1:9, pl.ds(pl.multiple_of(v * 32 + 32, 32), 32), :].reshape(256, 256)
        return pred + lax.dot_general(a, whe[v], NT, preferred_element_type=f32)

    pred = lax.fori_loop(0, 8, predict, jnp.zeros((256, 128), f32), unroll=HU)
    err = ((pred - heat_s[...]) * jnp.concatenate([weight_ref[...]] * 8, axis=0)).astype(bf16)
    err_s[...] = err
    err_t[...] = err.T
    bsum[...] = jnp.zeros_like(bsum)

    def spread(v, gh):
        at = pl.ds(pl.multiple_of(v * 32 + 32, 32), 32)
        a = act[2, 1:9, at, :].reshape(256, 256)
        d = jnp.where(a > 0, dot(err_s[...], whe[v]), 0.0).astype(bf16)
        bsum[2:3, :] += jnp.sum(d.astype(f32), axis=0, keepdims=True)
        grad[2, 1:9, at, :] = d.reshape(8, 32, 256)
        return gh + dot(err_t[block(v, 16), :], a)

    gh = lax.fori_loop(0, 8, spread, jnp.zeros((16, 256), f32), unroll=HV)
    ghead_ref[...] = gh.astype(bf16)
    base_ref[ROW_HEAD:ROW_HEAD + 16, :] = 0.5 * head_ref[...] - 0.1 * gh

    m = 8 // UB

    @pl.loop(0, 2 * m)
    def _(k):
        q = k // m
        s = 1 - q
        u = (k - q * m) * UB
        if ONE:
            order = [(i, j) for i in range(3) for j in range(3)]
            rows = [jnp.concatenate([grad[s + 1, u + e + 2 - i, (2 - j) * 32:(2 - j) * 32 + 256, :] for i, j in order], axis=1)
                    for e in range(UB)]
            lhs = rows[0] if UB == 1 else jnp.concatenate(rows, axis=0)
            w = jnp.concatenate(
                [wb[pl.ds(pl.multiple_of(s * 2304 + (3 * i + j) * 256, 256), 256), :] for i, j in order], axis=1)
            da = lax.dot_general(lhs, w, NT, preferred_element_type=f32)
        else:
            da = None
            for i in range(3):
                for j in range(3):
                    ii, jj = 2 - i, 2 - j
                    rows = [grad[s + 1, u + e + ii, jj * 32:jj * 32 + 256, :] for e in range(UB)]
                    lhs = rows[0] if UB == 1 else jnp.concatenate(rows, axis=0)
                    w = wb[pl.ds(pl.multiple_of(s * 2304 + (3 * i + j) * 256, 256), 256), :]
                    t = lax.dot_general(lhs, w, NT, preferred_element_type=f32)
                    da = t if da is None else da + t
        keep = q.astype(f32)
        for e in range(UB):
            d = da[e * 256:(e + 1) * 256] + keep * grad[2, u + e + 1, 32:288, :].astype(f32)
            d = jnp.where(act[s, u + e + 1, 32:288, :] > 0, d, 0.0).astype(bf16)
            grad[s, u + e + 1, 32:288, :] = d
            bsum[pl.ds(s, 1), :] += jnp.sum(d.astype(f32), axis=0, keepdims=True)

    gbias_ref[...] = bsum[0:3, :].astype(bf16)
    base_ref[ROW_HEAD + 16:ROW_HEAD + 24, :] = 0.5 * jnp.concatenate([bias_ref[0], bias_ref[1], bias_ref[2], jnp.zeros((5, 256), f32)], axis=0) - 0.1 * bsum[...]
    base_ref[ROW_HEAD + 24:PACKED, :] = jnp.zeros((8, 256), f32)
    gs = dot(x_t[...], grad[0, 1:9, 32:288, :].reshape(2048, 256))
    gstem_ref[...] = gs.astype(bf16)
    base_ref[ROW_STEM:ROW_HEAD, :] = 0.5 * stem_ref[...] - 0.1 * gs

    load_mine.wait()

    def outs(t):
        r = block(t, 256)
        return (pltpu.make_async_copy(gb.at[r], gconv_hbm.at[r], gsem.at[t]),)

    @pl.loop(0, 6)
    def _(q):
        s = q // 3
        j = q - s * 3
        rhs = grad[s + 1, 1:9, 32:288, :].reshape(2048, 256)
        lhs = jnp.concatenate([act_t[s, j, :, i * 256:i * 256 + 2048] for i in range(3)], axis=0)
        all_rows = dot(lhs, rhs)
        for i in range(3):
            t = s * 9 + i * 3 + j
            g = all_rows[i * 256:(i + 1) * 256]
            r = block(t, 256)
            gb[r, :] = g.astype(bf16)
            base_ref[r, :] = 0.5 * mine[r, :] - 0.1 * g
            for c in outs(t):
                c.start()

    @pl.loop(0, 18)
    def _(t):
        for c in outs(t):
            c.wait()


def main_call(weight, sel, got, packed, bias, conv, stem, head, U=2, UB=2, HU=8, HV=4, ONE=False):
    vm = pl.BlockSpec(memory_space=pltpu.VMEM)
    hb = pl.BlockSpec(memory_space=pltpu.HBM)
    S = jax.ShapeDtypeStruct
    maps = pltpu.VMEM((3, 10, 320, 256), bf16)
    return pl.pallas_call(
        functools.partial(main_kernel, U=U, UB=UB, HU=HU, HV=HV, ONE=ONE),
        out_shape=(S((4608, 256), bf16), S((PACKED, 256), f32), S((128, 256), bf16), S((16, 256), bf16), S((3, 256), bf16)),
        in_specs=[vm, vm, vm, hb, vm, hb, vm, vm],
        out_specs=(hb, vm, vm, vm, vm),
        scratch_shapes=[
            pltpu.VMEM((PACKED, 256), bf16), pltpu.VMEM((4608, 256), f32), pltpu.VMEM((4608, 256), bf16),
            pltpu.VMEM((128, 2048), bf16), pltpu.VMEM((256, 128), f32), maps, pltpu.VMEM((2, 3, 256, 2560), bf16), maps,
            pltpu.VMEM((8, 128, 256), bf16), pltpu.VMEM((256, 128), bf16), pltpu.VMEM((128, 256), bf16),
            pltpu.VMEM((8, 256), f32),
            pltpu.SemaphoreType.DMA((2,)), pltpu.SemaphoreType.DMA, pltpu.SemaphoreType.DMA((18,)),
        ],
        compiler_params=pltpu.CompilerParams(vmem_limit_bytes=48 * 1024 * 1024),
        cost_estimate=pl.CostEstimate(flops=16_000_000_000, bytes_accessed=16_000_000, transcendentals=0),
    )(weight, sel, got, packed, bias, conv, stem, head)


BOTH = ("grp", "dev")
SAME_Z = [[y * 8 + z * 2 + c for y in range(4) for c in range(2)] for z in range(4)]
SAME_Y = [[y * 8 + z * 2 + c for z in range(4) for c in range(2)] for y in range(4)]
Y_BITS = (3, 4)


def prep_kernel(me_ref, step_ref, count_ref, req_hbm, home_hbm, maps_hbm, heat_hbm, asked_ref, sel_ref, weight_ref, mine_ref,
                req, home, heat, maps, wide, sems):
    copies = [
        pltpu.make_async_copy(src, dst, sems.at[k])
        for k, (src, dst) in enumerate((
            (maps_hbm, maps), (heat_hbm, heat), (req_hbm, req), (home_hbm, home),
        ))
    ]
    for c in copies:
        c.start()
    for c in copies[2:]:
        c.wait()
    count = count_ref[0]
    bit = step_ref[0] & 7
    on_y = ((bit == Y_BITS[0]) | (bit == Y_BITS[1])).astype(jnp.int32)
    i = lax.broadcasted_iota(jnp.int32, (32, 32), 0)
    j = lax.broadcasted_iota(jnp.int32, (32, 32), 1)
    wanted = jnp.sum(jnp.where(i == j, req[...], 0), axis=1, keepdims=True)
    lane = lax.broadcasted_iota(jnp.int32, (32, 256), 1)
    pos = jnp.sum(jnp.where(lane == wanted, home[...], 0), axis=1, keepdims=True)
    owner = pos >> 3
    along = 1 + 2 * on_y
    other = 4 - along
    here = (me_ref[0] >> along) & 3
    column = ((owner >> other) & 3) * 2 + (owner & 1)
    row = (((owner >> along) & 3) ^ here) * 8 + (pos & 7)
    across_lanes = jnp.sum(jnp.where(i == j, column, 0), axis=0, keepdims=True)
    live = lax.broadcasted_iota(jnp.int32, (32, 1), 0) < count
    earlier = (across_lanes == column) & (j < i) & (j < count)
    rank = jnp.minimum(jnp.sum(jnp.where(earlier, 1, 0), axis=1, keepdims=True), 7)
    lane64 = lax.broadcasted_iota(jnp.int32, (32, 64), 1)
    pick = jnp.where((lane64 == column * 8 + rank) & live, 1.0, 0.0)
    sel_ref[...] = pick.astype(bf16)
    total = jnp.full((32, 128), count * 1024, jnp.int32).astype(f32)
    weight_ref[...] = jnp.where(lax.broadcasted_iota(jnp.int32, (32, 128), 0) < count, 2.0 / total, 0.0)
    value = jnp.broadcast_to((row + 1).astype(f32), (32, 128)).astype(bf16)
    asked = lax.dot_general(pick.astype(bf16), value, TN, preferred_element_type=f32)
    asked_ref[...] = (asked.astype(jnp.int32) - 1).reshape(8, 8, 128)
    copies[0].wait()
    wide[...] = maps[...].reshape(512, 128).astype(f32)
    for p in range(64):
        mine_ref[:, p * 128:(p + 1) * 128] = wide[pl.ds(p, 8, stride=64), :].astype(bf16)
    copies[1].wait()
    mine_ref[:, 8192:9216] = heat[...]


def prep(me, number, count, req, home, maps, heat):
    vm = pl.BlockSpec(memory_space=pltpu.VMEM)
    sm = pl.BlockSpec(memory_space=pltpu.SMEM)
    hb = pl.BlockSpec(memory_space=pltpu.HBM)
    S = jax.ShapeDtypeStruct
    return pl.pallas_call(
        prep_kernel,
        out_shape=(S((8, 8, 128), jnp.int32), S((32, 64), bf16), S((32, 128), f32), S((8, 9216), bf16)),
        in_specs=[sm, sm, sm, hb, hb, hb, hb],
        out_specs=(vm, vm, vm, vm),
        scratch_shapes=[
            pltpu.VMEM((1, 32), jnp.int32),
            pltpu.VMEM((1, 256), jnp.int32),
            pltpu.VMEM((8, 1024), bf16),
            pltpu.VMEM((8, 64, 128), bf16),
            pltpu.VMEM((512, 128), f32),
            pltpu.SemaphoreType.DMA((4,)),
        ],
        compiler_params=pltpu.CompilerParams(vmem_limit_bytes=60 * 1024 * 1024),
    )(me, number, count, req, home, maps, heat)


def choose_kernel(table_hbm, *refs):
    piles, (out_ref, table, pile, sems) = refs[:4], refs[4:]
    copies = [pltpu.make_async_copy(table_hbm, table, sems.at[4])]
    copies += [pltpu.make_async_copy(p, pile.at[k], sems.at[k]) for k, p in enumerate(piles)]
    for c in copies:
        c.start()
    for c in copies:
        c.wait()
    lane = lax.broadcasted_iota(jnp.int32, (64, 32), 1)
    pick = jnp.where(table[:, 0:32] == lane, 1.0, 0.0).astype(bf16)

    @pl.loop(0, 9)
    def _(k):
        rows = jnp.concatenate([pile[p, :, block(k, 1024)] for p in range(4)], axis=0)
        out_ref[:, block(k, 1024)] = dot(pick, rows).astype(bf16)


def choose(table, *piles):
    hb = pl.BlockSpec(memory_space=pltpu.HBM)
    return pl.pallas_call(
        choose_kernel,
        out_shape=jax.ShapeDtypeStruct((64, 9216), bf16),
        in_specs=[hb] * 5,
        out_specs=pl.BlockSpec(memory_space=pltpu.VMEM),
        scratch_shapes=[
            pltpu.VMEM((64, 128), jnp.int32),
            pltpu.VMEM((4, 8, 9216), bf16),
            pltpu.SemaphoreType.DMA((5,)),
        ],
        compiler_params=pltpu.CompilerParams(vmem_limit_bytes=8 * 1024 * 1024),
        cost_estimate=pl.CostEstimate(flops=40000000, bytes_accessed=2000000, transcendentals=0),
    )(table, *piles)


PARTS = 6
PART = 4608 // PARTS


def pack_kernel(conv_hbm, stem_hbm, head_hbm, bias_hbm, out_hbm, wide, bias, narrow, isem, osem):
    def load(k):
        r = block(k, PART)
        return pltpu.make_async_copy(conv_hbm.at[r], wide.at[r], isem.at[k])

    def save(k):
        r = block(k, PART)
        return pltpu.make_async_copy(narrow.at[r], out_hbm.at[r], osem.at[k])

    def save_tail():
        r = pl.ds(ROW_STEM, 160)
        return pltpu.make_async_copy(narrow.at[r], out_hbm.at[r], osem.at[PARTS])

    small = [
        pltpu.make_async_copy(stem_hbm, wide.at[pl.ds(ROW_STEM, 128)], isem.at[PARTS]),
        pltpu.make_async_copy(head_hbm, wide.at[pl.ds(ROW_HEAD, 16)], isem.at[PARTS + 1]),
        pltpu.make_async_copy(bias_hbm, bias, isem.at[PARTS + 2]),
    ]
    for k in range(PARTS):
        load(k).start()
    for c in small:
        c.start()

    def narrowed(lo, n):
        @pl.loop(0, n // 48)
        def _(q):
            r = pl.ds(pl.multiple_of(lo + q * 48, 16), 48)
            narrow[r, :] = wide[r, :].astype(bf16)

    @pl.loop(0, PARTS)
    def _(k):
        load(k).wait()
        narrowed(k * PART, PART)
        save(k).start()

    for c in small:
        c.wait()
    narrowed(ROW_STEM, 144)
    narrow[ROW_STEM + 144:PACKED, :] = jnp.concatenate([bias[0], bias[1], bias[2], jnp.zeros((13, 256), f32)], axis=0).astype(bf16)
    save_tail().start()

    @pl.loop(0, PARTS)
    def _(k):
        save(k).wait()

    save_tail().wait()


def pack(conv, stem, head, bias):
    hb = pl.BlockSpec(memory_space=pltpu.HBM)
    return pl.pallas_call(
        pack_kernel,
        out_shape=jax.ShapeDtypeStruct((PACKED, 256), bf16),
        in_specs=[hb, hb, hb, hb],
        out_specs=hb,
        scratch_shapes=[
            pltpu.VMEM((PACKED, 256), f32),
            pltpu.VMEM((3, 1, 256), f32),
            pltpu.VMEM((PACKED, 256), bf16),
            pltpu.SemaphoreType.DMA((PARTS + 3,)),
            pltpu.SemaphoreType.DMA((PARTS + 1,)),
        ],
        compiler_params=pltpu.CompilerParams(vmem_limit_bytes=16 * 1024 * 1024),
        cost_estimate=pl.CostEstimate(flops=1000000, bytes_accessed=7000000, transcendentals=0),
    )(conv, stem, head, bias)


PIECES = ((0, 256), (256, 512), (768, 768), (1536, 1024), (2560, 1024), (3584, 640), (4224, 384))


def mix_kernel(t_hbm, base_ref, new_hbm, nstem_hbm, nhead_hbm, nbias_ref, theirs, wide, asem, osem):
    def load(k, lo, n):
        return pltpu.make_async_copy(t_hbm.at[pl.ds(lo, n)], theirs.at[pl.ds(lo, n)], asem.at[k])

    def mixed(lo, n, m):
        @pl.loop(0, n // m)
        def _(q):
            r = pl.ds(pl.multiple_of(lo + q * m, 32), m)
            wide[r, :] = base_ref[r, :] + 0.5 * theirs[r, :].astype(f32)

    loads = [load(k, lo, n) for k, (lo, n) in enumerate(PIECES + ((ROW_STEM, 160),))]
    for c in loads:
        c.start()
    saves = []
    for k, (lo, n) in enumerate(PIECES):
        loads[k].wait()
        mixed(lo, n, 128)
        saves.append(pltpu.make_async_copy(wide.at[pl.ds(lo, n)], new_hbm.at[pl.ds(lo, n)], osem.at[k]))
        saves[-1].start()
    loads[-1].wait()
    mixed(ROW_STEM, 160, 160)
    last = len(PIECES)
    saves.append(pltpu.make_async_copy(wide.at[pl.ds(ROW_STEM, 128)], nstem_hbm, osem.at[last]))
    saves.append(pltpu.make_async_copy(wide.at[pl.ds(ROW_HEAD, 16)], nhead_hbm, osem.at[last + 1]))
    for c in saves[-2:]:
        c.start()
    for k in range(3):
        nbias_ref[k] = wide[ROW_HEAD + 16 + k:ROW_HEAD + 17 + k, :]
    for c in saves:
        c.wait()


def mix(theirs, base):
    vm = pl.BlockSpec(memory_space=pltpu.VMEM)
    hb = pl.BlockSpec(memory_space=pltpu.HBM)
    S = jax.ShapeDtypeStruct
    return pl.pallas_call(
        mix_kernel,
        out_shape=(S((4608, 256), f32), S((128, 256), f32), S((16, 256), f32), S((3, 1, 256), f32)),
        in_specs=[hb, vm],
        out_specs=(hb, hb, hb, vm),
        scratch_shapes=[
            pltpu.VMEM((PACKED, 256), bf16),
            pltpu.VMEM((PACKED, 256), f32),
            pltpu.SemaphoreType.DMA((len(PIECES) + 1,)),
            pltpu.SemaphoreType.DMA((len(PIECES) + 2,)),
        ],
        compiler_params=pltpu.CompilerParams(vmem_limit_bytes=24 * 1024 * 1024),
        cost_estimate=pl.CostEstimate(flops=1000000, bytes_accessed=12000000, transcendentals=0),
    )(theirs, base)


def swap(array, bit):
    return lax.ppermute(array, BOTH, [(i, i ^ (1 << bit)) for i in range(256)])


def among(array, groups):
    return lax.all_to_all(array, "dev", split_axis=0, concat_axis=0, axis_index_groups=groups, tiled=True)


def gather(on_y, asked, mine, conv, stem, head, bias):
    shift, groups = (3, SAME_Y) if on_y else (1, SAME_Z)
    others = [lax.ppermute(mine, "dev", [(i, i ^ (m << shift)) for i in range(32)]) for m in (1, 2, 3)]
    table = among(asked, groups)
    packed = pack(conv, stem, head, bias)
    return packed, table, *others


def step(bit, weight, sel, table, mine, one, two, three, packed, bias, conv, stem, head):
    theirs = swap(packed, bit)
    send = choose(table.reshape(64, 128), mine, one, two, three).reshape(8, 8, 9216)
    got = among(send, SAME_Y if bit in Y_BITS else SAME_Z)
    outs = main_call(weight, sel, got.reshape(64, 9216), packed, bias, conv, stem, head)
    return (theirs, *outs)


def local(step_number, maps, heat, home, requests, counts, stem, conv, head, bias):
    stem, conv, head, bias = stem[0], conv.reshape(4608, 256), head[0], jnp.transpose(bias, (1, 0, 2))
    bit = step_number & 7
    on_y = ((bit == Y_BITS[0]) | (bit == Y_BITS[1])).astype(jnp.int32)
    me = lax.axis_index("dev").astype(jnp.int32)
    asked, sel, weight, mine = prep(me.reshape(1), step_number.reshape(1), counts, requests, home, maps, heat)
    packed, table, *others = lax.switch(
        on_y, [functools.partial(gather, 0), functools.partial(gather, 1)],
        asked, mine, conv, stem, head, bias,
    )
    outs = lax.switch(
        bit, [functools.partial(step, b) for b in range(8)],
        weight, sel, table, mine, *others, packed, bias, conv, stem, head,
    )
    theirs, gconv, base, gstem, ghead, gbias = outs
    new, nstem, nhead, nbias = mix(theirs, base)
    return (
        nstem[None], new.reshape(1, 2, 2304, 256), nhead[None], jnp.transpose(nbias, (1, 0, 2)),
        gstem[None], gconv.reshape(1, 2, 2304, 256), ghead[None], gbias[None],
    )


def solution(mesh):
    placed = (
        P(),
        P(BOTH, None, None),
        P(BOTH, None),
        P("grp", None),
        P(BOTH, None),
        P(BOTH),
        P(BOTH, None, None),
        P(BOTH, None, None, None),
        P(BOTH, None, None),
        P(BOTH, None, None),
    )
    outs = (
        P(BOTH, None, None),
        P(BOTH, None, None, None),
        P(BOTH, None, None),
        P(BOTH, None, None),
        P(BOTH, None, None),
        P(BOTH, None, None, None),
        P(BOTH, None, None),
        P(BOTH, None, None),
    )
    return jax.shard_map(local, mesh=mesh, in_specs=placed, out_specs=outs, check_vma=False)
```

```python
import functools

import jax
import jax.numpy as jnp
from jax import lax
from jax.experimental import pallas as pl
from jax.experimental.pallas import tpu as pltpu
from jax.sharding import PartitionSpec as P


bf16 = jnp.bfloat16
f32 = jnp.float32
NT = (((1,), (1,)), ((), ()))
TN = (((0,), (0,)), ((), ()))
ROW_STEM = 4608
ROW_HEAD = 4736
PACKED = 4768


def dot(a, b):
    return jnp.dot(a, b, preferred_element_type=f32)


def block(i, n):
    return pl.ds(pl.multiple_of(i * n, n), n)


def main_kernel(
    weight_ref, sel_ref, got_ref, w_hbm, bias_ref, conv_hbm, stem_ref, head_ref,
    gconv_hbm, base_ref, gstem_ref, ghead_ref, gbias_ref,
    wb, mine, gb, x_t, heat_s, act, act_t, grad, whe, err_s, err_t, bsum,
    wsem, msem, gsem, *, U, UB, HU, HV, ONE):
    wcopies = []
    for k, (lo, n) in enumerate(((ROW_STEM, PACKED - ROW_STEM), (0, ROW_STEM))):
        c = pltpu.make_async_copy(w_hbm.at[pl.ds(lo, n)], wb.at[pl.ds(lo, n)], wsem.at[k])
        c.start()
        wcopies.append(c)
    load_mine = pltpu.make_async_copy(conv_hbm, mine, msem)

    edge = jnp.zeros((32, 256), bf16)

    @pl.loop(0, 10)
    def _(q):
        for buf, ks in ((act, (0, 1)), (grad, (1, 2))):
            for k in ks:
                buf[k, 0, block(q, 32), :] = edge
                buf[k, 9, block(q, 32), :] = edge
                buf[k, q, 0:32, :] = edge
                buf[k, q, 288:320, :] = edge

    @pl.loop(0, 6)
    def _(q):
        z = jnp.zeros((256, 256), bf16)
        act_t[q // 3, q % 3, :, 0:256] = z
        act_t[q // 3, q % 3, :, 2304:2560] = z

    sel = sel_ref[...]
    wcopies[0].wait()
    ws = wb[ROW_STEM:ROW_STEM + 128, :]
    b0 = bias_ref[0]

    @pl.loop(0, 8)
    def _(u):
        r = dot(sel, got_ref[:, block(u, 1024)]).astype(bf16)
        x = jnp.concatenate([r[:, v * 128:(v + 1) * 128] for v in range(8)], axis=0)
        x_t[:, block(u, 256)] = x.T
        heat_s[block(u, 32), :] = dot(sel, got_ref[:, pl.ds(pl.multiple_of(8192 + u * 128, 128), 128)])
        pre = dot(x, ws) + b0
        a = jnp.maximum(pre, 0.0).astype(bf16)
        act[0, u + 1, 32:288, :] = a

    wcopies[1].wait()
    load_mine.start()
    n = 8 // U

    @pl.loop(0, 2 * n)
    def _(k):
        s = k // n
        u = (k - s * n) * U
        rows = []
        for e in range(U):
            rows.append(jnp.concatenate(
                [act[s, u + e + i, j * 32:j * 32 + 256, :] for i in range(3) for j in range(3)], axis=1))
        lhs = rows[0] if U == 1 else jnp.concatenate(rows, axis=0)
        pre = dot(lhs, wb[block(s, 2304), :]) + bias_ref[s + 1]
        for e in range(U):
            for j in range(3):
                act_t[s, j, :, block(u + e + 1, 256)] = act[s, u + e + 1, j * 32:j * 32 + 256, :].T
        keep = s.astype(f32)
        for e in range(U):
            p = pre[e * 256:(e + 1) * 256] + keep * act[0, u + e + 1, 32:288, :].astype(f32)
            a = jnp.maximum(p, 0.0).astype(bf16)
            act[s + 1, u + e + 1, 32:288, :] = a

    wh = wb[ROW_HEAD:ROW_HEAD + 16, :]

    def predict(v, pred):
        whe[v] = jnp.zeros((128, 256), bf16)
        whe[v, block(v, 16), :] = wh
        a = act[2, 1:9, pl.ds(pl.multiple_of(v * 32 + 32, 32), 32), :].reshape(256, 256)
        return pred + lax.dot_general(a, whe[v], NT, preferred_element_type=f32)

    pred = lax.fori_loop(0, 8, predict, jnp.zeros((256, 128), f32), unroll=HU)
    err = ((pred - heat_s[...]) * jnp.concatenate([weight_ref[...]] * 8, axis=0)).astype(bf16)
    err_s[...] = err
    err_t[...] = err.T
    bsum[...] = jnp.zeros_like(bsum)

    def spread(v, gh):
        at = pl.ds(pl.multiple_of(v * 32 + 32, 32), 32)
        a = act[2, 1:9, at, :].reshape(256, 256)
        d = jnp.where(a > 0, dot(err_s[...], whe[v]), 0.0).astype(bf16)
        bsum[2:3, :] += jnp.sum(d.astype(f32), axis=0, keepdims=True)
        grad[2, 1:9, at, :] = d.reshape(8, 32, 256)
        return gh + dot(err_t[block(v, 16), :], a)

    gh = lax.fori_loop(0, 8, spread, jnp.zeros((16, 256), f32), unroll=HV)
    ghead_ref[...] = gh.astype(bf16)
    base_ref[ROW_HEAD:ROW_HEAD + 16, :] = 0.5 * head_ref[...] - 0.1 * gh

    m = 8 // UB

    @pl.loop(0, 2 * m)
    def _(k):
        q = k // m
        s = 1 - q
        u = (k - q * m) * UB
        if ONE:
            order = [(i, j) for i in range(3) for j in range(3)]
            rows = [jnp.concatenate([grad[s + 1, u + e + 2 - i, (2 - j) * 32:(2 - j) * 32 + 256, :] for i, j in order], axis=1)
                    for e in range(UB)]
            lhs = rows[0] if UB == 1 else jnp.concatenate(rows, axis=0)
            w = jnp.concatenate(
                [wb[pl.ds(pl.multiple_of(s * 2304 + (3 * i + j) * 256, 256), 256), :] for i, j in order], axis=1)
            da = lax.dot_general(lhs, w, NT, preferred_element_type=f32)
        else:
            da = None
            for i in range(3):
                for j in range(3):
                    ii, jj = 2 - i, 2 - j
                    rows = [grad[s + 1, u + e + ii, jj * 32:jj * 32 + 256, :] for e in range(UB)]
                    lhs = rows[0] if UB == 1 else jnp.concatenate(rows, axis=0)
                    w = wb[pl.ds(pl.multiple_of(s * 2304 + (3 * i + j) * 256, 256), 256), :]
                    t = lax.dot_general(lhs, w, NT, preferred_element_type=f32)
                    da = t if da is None else da + t
        keep = q.astype(f32)
        for e in range(UB):
            d = da[e * 256:(e + 1) * 256] + keep * grad[2, u + e + 1, 32:288, :].astype(f32)
            d = jnp.where(act[s, u + e + 1, 32:288, :] > 0, d, 0.0).astype(bf16)
            grad[s, u + e + 1, 32:288, :] = d
            bsum[pl.ds(s, 1), :] += jnp.sum(d.astype(f32), axis=0, keepdims=True)

    gbias_ref[...] = bsum[0:3, :].astype(bf16)
    base_ref[ROW_HEAD + 16:ROW_HEAD + 24, :] = 0.5 * jnp.concatenate([bias_ref[0], bias_ref[1], bias_ref[2], jnp.zeros((5, 256), f32)], axis=0) - 0.1 * bsum[...]
    base_ref[ROW_HEAD + 24:PACKED, :] = jnp.zeros((8, 256), f32)
    gs = dot(x_t[...], grad[0, 1:9, 32:288, :].reshape(2048, 256))
    gstem_ref[...] = gs.astype(bf16)
    base_ref[ROW_STEM:ROW_HEAD, :] = 0.5 * stem_ref[...] - 0.1 * gs

    load_mine.wait()

    def outs(t):
        r = block(t, 256)
        return (pltpu.make_async_copy(gb.at[r], gconv_hbm.at[r], gsem.at[t]),)

    @pl.loop(0, 6)
    def _(q):
        s = q // 3
        j = q - s * 3
        rhs = grad[s + 1, 1:9, 32:288, :].reshape(2048, 256)
        lhs = jnp.concatenate([act_t[s, j, :, i * 256:i * 256 + 2048] for i in range(3)], axis=0)
        all_rows = dot(lhs, rhs)
        for i in range(3):
            t = s * 9 + i * 3 + j
            g = all_rows[i * 256:(i + 1) * 256]
            r = block(t, 256)
            gb[r, :] = g.astype(bf16)
            base_ref[r, :] = 0.5 * mine[r, :] - 0.1 * g
            for c in outs(t):
                c.start()

    @pl.loop(0, 18)
    def _(t):
        for c in outs(t):
            c.wait()


def main_call(weight, sel, got, packed, bias, conv, stem, head, U=2, UB=2, HU=8, HV=2, ONE=False):
    vm = pl.BlockSpec(memory_space=pltpu.VMEM)
    hb = pl.BlockSpec(memory_space=pltpu.HBM)
    S = jax.ShapeDtypeStruct
    maps = pltpu.VMEM((3, 10, 320, 256), bf16)
    return pl.pallas_call(
        functools.partial(main_kernel, U=U, UB=UB, HU=HU, HV=HV, ONE=ONE),
        out_shape=(S((4608, 256), bf16), S((PACKED, 256), f32), S((128, 256), bf16), S((16, 256), bf16), S((3, 256), bf16)),
        in_specs=[vm, vm, vm, hb, vm, hb, vm, vm],
        out_specs=(hb, vm, vm, vm, vm),
        scratch_shapes=[
            pltpu.VMEM((PACKED, 256), bf16), pltpu.VMEM((4608, 256), f32), pltpu.VMEM((4608, 256), bf16),
            pltpu.VMEM((128, 2048), bf16), pltpu.VMEM((256, 128), f32), maps, pltpu.VMEM((2, 3, 256, 2560), bf16), maps,
            pltpu.VMEM((8, 128, 256), bf16), pltpu.VMEM((256, 128), bf16), pltpu.VMEM((128, 256), bf16),
            pltpu.VMEM((8, 256), f32),
            pltpu.SemaphoreType.DMA((2,)), pltpu.SemaphoreType.DMA, pltpu.SemaphoreType.DMA((18,)),
        ],
        compiler_params=pltpu.CompilerParams(vmem_limit_bytes=48 * 1024 * 1024),
        cost_estimate=pl.CostEstimate(flops=16_000_000_000, bytes_accessed=16_000_000, transcendentals=0),
    )(weight, sel, got, packed, bias, conv, stem, head)


BOTH = ("grp", "dev")
SAME_Z = [[y * 8 + z * 2 + c for y in range(4) for c in range(2)] for z in range(4)]
SAME_Y = [[y * 8 + z * 2 + c for z in range(4) for c in range(2)] for y in range(4)]
Y_BITS = (3, 4)


def spread_kernel(maps_hbm, heat_hbm, mine_ref, heat, maps, wide, sems):
    copies = [pltpu.make_async_copy(maps_hbm, maps, sems.at[0]), pltpu.make_async_copy(heat_hbm, heat, sems.at[1])]
    for c in copies:
        c.start()
    copies[0].wait()
    wide[...] = maps[...].reshape(512, 128).astype(f32)
    for p in range(64):
        mine_ref[:, p * 128:(p + 1) * 128] = wide[pl.ds(p, 8, stride=64), :].astype(bf16)
    copies[1].wait()
    mine_ref[:, 8192:9216] = heat[...]


def spread(maps, heat):
    vm = pl.BlockSpec(memory_space=pltpu.VMEM)
    hb = pl.BlockSpec(memory_space=pltpu.HBM)
    return pl.pallas_call(
        spread_kernel,
        out_shape=jax.ShapeDtypeStruct((8, 9216), bf16),
        in_specs=[hb, hb],
        out_specs=vm,
        scratch_shapes=[
            pltpu.VMEM((8, 1024), bf16),
            pltpu.VMEM((8, 64, 128), bf16),
            pltpu.VMEM((512, 128), f32),
            pltpu.SemaphoreType.DMA((2,)),
        ],
        compiler_params=pltpu.CompilerParams(vmem_limit_bytes=60 * 1024 * 1024),
    )(maps, heat)


def route_kernel(along, me_ref, count_ref, req_hbm, home_hbm, asked_ref, sel_ref, weight_ref, req, home, sems):
    copies = [pltpu.make_async_copy(req_hbm, req, sems.at[0]), pltpu.make_async_copy(home_hbm, home, sems.at[1])]
    for c in copies:
        c.start()
    for c in copies:
        c.wait()
    count = count_ref[0]
    i = lax.broadcasted_iota(jnp.int32, (32, 32), 0)
    j = lax.broadcasted_iota(jnp.int32, (32, 32), 1)
    wanted = jnp.sum(jnp.where(i == j, req[...], 0), axis=1, keepdims=True)
    lane = lax.broadcasted_iota(jnp.int32, (32, 256), 1)
    pos = jnp.sum(jnp.where(lane == wanted, home[...], 0), axis=1, keepdims=True)
    owner = pos >> 3
    here = (me_ref[0] >> along) & 3
    column = ((owner >> (4 - along)) & 3) * 2 + (owner & 1)
    row = (((owner >> along) & 3) ^ here) * 8 + (pos & 7)
    across_lanes = jnp.sum(jnp.where(i == j, column, 0), axis=0, keepdims=True)
    live = lax.broadcasted_iota(jnp.int32, (32, 1), 0) < count
    earlier = (across_lanes == column) & (j < i) & (j < count)
    rank = jnp.minimum(jnp.sum(jnp.where(earlier, 1, 0), axis=1, keepdims=True), 7)
    lane64 = lax.broadcasted_iota(jnp.int32, (32, 64), 1)
    pick = jnp.where((lane64 == column * 8 + rank) & live, 1.0, 0.0)
    sel_ref[...] = pick.astype(bf16)
    total = jnp.full((32, 128), count * 1024, jnp.int32).astype(f32)
    weight_ref[...] = jnp.where(lax.broadcasted_iota(jnp.int32, (32, 128), 0) < count, 2.0 / total, 0.0)
    value = jnp.broadcast_to((row + 1).astype(f32), (32, 128)).astype(bf16)
    asked = lax.dot_general(pick.astype(bf16), value, TN, preferred_element_type=f32)
    asked_ref[...] = (asked.astype(jnp.int32) - 1).reshape(8, 8, 128)


def route(along, me, count, req, home):
    vm = pl.BlockSpec(memory_space=pltpu.VMEM)
    sm = pl.BlockSpec(memory_space=pltpu.SMEM)
    hb = pl.BlockSpec(memory_space=pltpu.HBM)
    S = jax.ShapeDtypeStruct
    return pl.pallas_call(
        functools.partial(route_kernel, along),
        out_shape=(S((8, 8, 128), jnp.int32), S((32, 64), bf16), S((32, 128), f32)),
        in_specs=[sm, sm, hb, hb],
        out_specs=(vm, vm, vm),
        scratch_shapes=[pltpu.VMEM((1, 32), jnp.int32), pltpu.VMEM((1, 256), jnp.int32), pltpu.SemaphoreType.DMA((2,))],
        compiler_params=pltpu.CompilerParams(vmem_limit_bytes=8 * 1024 * 1024),
        cost_estimate=pl.CostEstimate(flops=1000000, bytes_accessed=100000, transcendentals=0),
    )(me, count, req, home)


def choose_kernel(table_hbm, *refs):
    piles, (out_ref, table, pile, sems) = refs[:4], refs[4:]
    copies = [pltpu.make_async_copy(table_hbm, table, sems.at[4])]
    copies += [pltpu.make_async_copy(p, pile.at[k], sems.at[k]) for k, p in enumerate(piles)]
    for c in copies:
        c.start()
    for c in copies:
        c.wait()
    lane = lax.broadcasted_iota(jnp.int32, (64, 32), 1)
    pick = jnp.where(table[:, 0:32] == lane, 1.0, 0.0).astype(bf16)

    @pl.loop(0, 9)
    def _(k):
        rows = jnp.concatenate([pile[p, :, block(k, 1024)] for p in range(4)], axis=0)
        out_ref[:, block(k, 1024)] = dot(pick, rows).astype(bf16)


def choose(table, *piles):
    hb = pl.BlockSpec(memory_space=pltpu.HBM)
    return pl.pallas_call(
        choose_kernel,
        out_shape=jax.ShapeDtypeStruct((64, 9216), bf16),
        in_specs=[hb] * 5,
        out_specs=pl.BlockSpec(memory_space=pltpu.VMEM),
        scratch_shapes=[
            pltpu.VMEM((64, 128), jnp.int32),
            pltpu.VMEM((4, 8, 9216), bf16),
            pltpu.SemaphoreType.DMA((5,)),
        ],
        compiler_params=pltpu.CompilerParams(vmem_limit_bytes=8 * 1024 * 1024),
        cost_estimate=pl.CostEstimate(flops=40000000, bytes_accessed=2000000, transcendentals=0),
    )(table, *piles)


PARTS = 6
PART = 4608 // PARTS


def pack_kernel(conv_hbm, stem_hbm, head_hbm, bias_hbm, out_hbm, wide, bias, narrow, isem, osem):
    def load(k):
        r = block(k, PART)
        return pltpu.make_async_copy(conv_hbm.at[r], wide.at[r], isem.at[k])

    def save(k):
        r = block(k, PART)
        return pltpu.make_async_copy(narrow.at[r], out_hbm.at[r], osem.at[k])

    def save_tail():
        r = pl.ds(ROW_STEM, 160)
        return pltpu.make_async_copy(narrow.at[r], out_hbm.at[r], osem.at[PARTS])

    small = [
        pltpu.make_async_copy(stem_hbm, wide.at[pl.ds(ROW_STEM, 128)], isem.at[PARTS]),
        pltpu.make_async_copy(head_hbm, wide.at[pl.ds(ROW_HEAD, 16)], isem.at[PARTS + 1]),
        pltpu.make_async_copy(bias_hbm, bias, isem.at[PARTS + 2]),
    ]
    for k in range(PARTS):
        load(k).start()
    for c in small:
        c.start()

    def narrowed(lo, n):
        @pl.loop(0, n // 48)
        def _(q):
            r = pl.ds(pl.multiple_of(lo + q * 48, 16), 48)
            narrow[r, :] = wide[r, :].astype(bf16)

    @pl.loop(0, PARTS)
    def _(k):
        load(k).wait()
        narrowed(k * PART, PART)
        save(k).start()

    for c in small:
        c.wait()
    narrowed(ROW_STEM, 144)
    narrow[ROW_STEM + 144:PACKED, :] = jnp.concatenate([bias[0], bias[1], bias[2], jnp.zeros((13, 256), f32)], axis=0).astype(bf16)
    save_tail().start()

    @pl.loop(0, PARTS)
    def _(k):
        save(k).wait()

    save_tail().wait()


def pack(conv, stem, head, bias):
    hb = pl.BlockSpec(memory_space=pltpu.HBM)
    return pl.pallas_call(
        pack_kernel,
        out_shape=jax.ShapeDtypeStruct((PACKED, 256), bf16),
        in_specs=[hb, hb, hb, hb],
        out_specs=hb,
        scratch_shapes=[
            pltpu.VMEM((PACKED, 256), f32),
            pltpu.VMEM((3, 1, 256), f32),
            pltpu.VMEM((PACKED, 256), bf16),
            pltpu.SemaphoreType.DMA((PARTS + 3,)),
            pltpu.SemaphoreType.DMA((PARTS + 1,)),
        ],
        compiler_params=pltpu.CompilerParams(vmem_limit_bytes=16 * 1024 * 1024),
        cost_estimate=pl.CostEstimate(flops=1000000, bytes_accessed=7000000, transcendentals=0),
    )(conv, stem, head, bias)


PIECES = ((0, 256), (256, 512), (768, 768), (1536, 1024), (2560, 1024), (3584, 640), (4224, 384))


def mix_kernel(t_hbm, base_ref, new_hbm, nstem_hbm, nhead_hbm, nbias_ref, theirs, wide, asem, osem):
    def load(k, lo, n):
        return pltpu.make_async_copy(t_hbm.at[pl.ds(lo, n)], theirs.at[pl.ds(lo, n)], asem.at[k])

    def mixed(lo, n, m):
        @pl.loop(0, n // m)
        def _(q):
            r = pl.ds(pl.multiple_of(lo + q * m, 32), m)
            wide[r, :] = base_ref[r, :] + 0.5 * theirs[r, :].astype(f32)

    loads = [load(k, lo, n) for k, (lo, n) in enumerate(PIECES + ((ROW_STEM, 160),))]
    for c in loads:
        c.start()
    saves = []
    for k, (lo, n) in enumerate(PIECES):
        loads[k].wait()
        mixed(lo, n, 128)
        saves.append(pltpu.make_async_copy(wide.at[pl.ds(lo, n)], new_hbm.at[pl.ds(lo, n)], osem.at[k]))
        saves[-1].start()
    loads[-1].wait()
    mixed(ROW_STEM, 160, 160)
    last = len(PIECES)
    saves.append(pltpu.make_async_copy(wide.at[pl.ds(ROW_STEM, 128)], nstem_hbm, osem.at[last]))
    saves.append(pltpu.make_async_copy(wide.at[pl.ds(ROW_HEAD, 16)], nhead_hbm, osem.at[last + 1]))
    for c in saves[-2:]:
        c.start()
    for k in range(3):
        nbias_ref[k] = wide[ROW_HEAD + 16 + k:ROW_HEAD + 17 + k, :]
    for c in saves:
        c.wait()


def mix(theirs, base):
    vm = pl.BlockSpec(memory_space=pltpu.VMEM)
    hb = pl.BlockSpec(memory_space=pltpu.HBM)
    S = jax.ShapeDtypeStruct
    return pl.pallas_call(
        mix_kernel,
        out_shape=(S((4608, 256), f32), S((128, 256), f32), S((16, 256), f32), S((3, 1, 256), f32)),
        in_specs=[hb, vm],
        out_specs=(hb, hb, hb, vm),
        scratch_shapes=[
            pltpu.VMEM((PACKED, 256), bf16),
            pltpu.VMEM((PACKED, 256), f32),
            pltpu.SemaphoreType.DMA((len(PIECES) + 1,)),
            pltpu.SemaphoreType.DMA((len(PIECES) + 2,)),
        ],
        compiler_params=pltpu.CompilerParams(vmem_limit_bytes=24 * 1024 * 1024),
        cost_estimate=pl.CostEstimate(flops=1000000, bytes_accessed=12000000, transcendentals=0),
    )(theirs, base)


def swap(array, bit):
    return lax.ppermute(array, BOTH, [(i, i ^ (1 << bit)) for i in range(256)])


def among(array, groups):
    return lax.all_to_all(array, "dev", split_axis=0, concat_axis=0, axis_index_groups=groups, tiled=True)


def gather(on_y, me, counts, requests, home, mine, conv, stem, head, bias):
    shift, groups = (3, SAME_Y) if on_y else (1, SAME_Z)
    others = [lax.ppermute(mine, "dev", [(i, i ^ (m << shift)) for i in range(32)]) for m in (1, 2, 3)]
    asked, sel, weight = route(shift, me, counts, requests, home)
    table = among(asked, groups)
    packed = pack(conv, stem, head, bias)
    return packed, sel, weight, table, *others


def step(bit, weight, sel, table, mine, one, two, three, packed, bias, conv, stem, head):
    theirs = swap(packed, bit)
    send = choose(table.reshape(64, 128), mine, one, two, three).reshape(8, 8, 9216)
    got = among(send, SAME_Y if bit in Y_BITS else SAME_Z)
    outs = main_call(weight, sel, got.reshape(64, 9216), packed, bias, conv, stem, head)
    return (theirs, *outs)


def local(step_number, maps, heat, home, requests, counts, stem, conv, head, bias):
    stem, conv, head, bias = stem[0], conv.reshape(4608, 256), head[0], jnp.transpose(bias, (1, 0, 2))
    bit = step_number & 7
    on_y = ((bit == Y_BITS[0]) | (bit == Y_BITS[1])).astype(jnp.int32)
    me = lax.axis_index("dev").astype(jnp.int32)
    mine = spread(maps, heat)
    packed, sel, weight, table, *others = lax.switch(
        on_y, [functools.partial(gather, 0), functools.partial(gather, 1)],
        me.reshape(1), counts, requests, home, mine, conv, stem, head, bias,
    )
    outs = lax.switch(
        bit, [functools.partial(step, b) for b in range(8)],
        weight, sel, table, mine, *others, packed, bias, conv, stem, head,
    )
    theirs, gconv, base, gstem, ghead, gbias = outs
    new, nstem, nhead, nbias = mix(theirs, base)
    return (
        nstem[None], new.reshape(1, 2, 2304, 256), nhead[None], jnp.transpose(nbias, (1, 0, 2)),
        gstem[None], gconv.reshape(1, 2, 2304, 256), ghead[None], gbias[None],
    )


def solution(mesh):
    placed = (
        P(),
        P(BOTH, None, None),
        P(BOTH, None),
        P("grp", None),
        P(BOTH, None),
        P(BOTH),
        P(BOTH, None, None),
        P(BOTH, None, None, None),
        P(BOTH, None, None),
        P(BOTH, None, None),
    )
    outs = (
        P(BOTH, None, None),
        P(BOTH, None, None, None),
        P(BOTH, None, None),
        P(BOTH, None, None),
        P(BOTH, None, None),
        P(BOTH, None, None, None),
        P(BOTH, None, None),
        P(BOTH, None, None),
    )
    return jax.shard_map(local, mesh=mesh, in_specs=placed, out_specs=outs, check_vma=False)
```
